256 devices in a mesh: grp: 4 (over z_lo, core), wide: 64 (over y, x, z_hi).
Axes of the slice: x: 4, y: 4, z: 8 (z_hi: 4, z_lo: 2; z = z_hi * 2 + z_lo), core: 2. Of those that a mesh axis runs over, the one named last changes fastest.
Arguments:
- acts: float32 [16384, 2048], P('wide'), may hold values from -6 to 6
- dec_bias: float32 [2048], replicated, may hold values from -2 to 2
- enc_weight: bfloat16 [4096, 2048], P(('grp', 'wide')), may hold values from -0.125 to 0.125
- enc_bias: bfloat16 [4096], P(('grp', 'wide')), may hold values from -3 to 3
- dec_weight: bfloat16 [4096, 2048], P(('grp', 'wide')), may hold values from -0.09375 to 0.09375
Outputs:
- recon: bfloat16 [16384, 2048], P('wide')
- grad_enc: float32 [4096, 2048], P(('grp', 'wide'))
- grad_dec: float32 [4096, 2048], P(('grp', 'wide'))
- grad_bias: float32 [4096], P(('grp', 'wide'))
The draws below stay inside these ranges and needn't reach their ends.
All inputs are finite; a program needn't handle non-finite values.
Results may differ from the reference program's by a relative error of at most 0.0055.
Values may be sent and summed in bfloat16 or wider, within the bound.
A program may use at most 64 MiB of HBM per device.

```python
import jax
import jax.numpy as jnp
from jax import lax

D = 2048
ROWS = 16384
GROUP_LAT = 1024
LATENTS = 4096
N_GRP = 4


def shard_levels(rng, extent, pieces, low, high):
    level = 1.0
    for dim, blocks in pieces:
        heights = jax.random.uniform(jax.random.fold_in(jax.random.fold_in(rng, 6), dim), (blocks,), jnp.float32, low / len(pieces), high / len(pieces))
        level = level * jnp.repeat(jnp.exp(heights), extent[dim] // blocks).reshape((-1,) + (1,) * (len(extent) - 1 - dim))
    return level


def noise(own_key, extent, width, most, shards=(), kind=jnp.bfloat16):
    entries = width * jax.random.normal(own_key, extent, jnp.float32)
    if shards:
        entries = entries * shard_levels(own_key, extent, shards, -0.22, 0.18)
    return jnp.clip(entries, -most, most).astype(kind)


def setup_inputs(seed: int = 0) -> dict:
    arg_keys = jax.random.split(jax.random.key(seed), 6)
    return {
        "acts": noise(arg_keys[0], (ROWS, D), 1.0, 6.0, ((0, 64),), jnp.float32),
        "dec_bias": noise(arg_keys[1], (D,), 0.3, 2.0, (), jnp.float32),
        "enc_weight": noise(arg_keys[2], (LATENTS, D), D ** -0.5, 0.125, ((0, 256),)),
        "enc_bias": noise(arg_keys[3], (LATENTS,), 0.5, 3.0, ((0, 256),)),
        "dec_weight": noise(arg_keys[4], (LATENTS, D), LATENTS ** -0.5, 0.09375, ((0, 256),)),
    }


sparsity_weight = 0.5

def encode(centered, enc_rows, enc_shift):
    pre = lax.dot_general(centered, enc_rows, (((1,), (1,)), ((), ())), preferred_element_type=jnp.float32)
    return pre + enc_shift.astype(jnp.float32)[None, :]

def reference(acts, dec_bias, enc_weight, enc_bias, dec_weight):
    centered = (acts - dec_bias[None, :]).astype(jnp.bfloat16)
    enc_groups = enc_weight.reshape(N_GRP, GROUP_LAT, D)
    bias_groups = enc_bias.reshape(N_GRP, GROUP_LAT)
    dec_groups = dec_weight.reshape(N_GRP, GROUP_LAT, D)

    def add_group(total, items):
        enc_rows, enc_shift, dec_rows = items
        codes_bf = jnp.maximum(encode(centered, enc_rows, enc_shift), 0.0).astype(jnp.bfloat16)
        return (total + jnp.dot(codes_bf, dec_rows, preferred_element_type=jnp.float32), None)
    summed, _ = lax.scan(add_group, jnp.zeros((ROWS, D), jnp.float32), (enc_groups, bias_groups, dec_groups))
    recon_full = summed + dec_bias[None, :]
    recon = recon_full.astype(jnp.bfloat16)
    error = (recon_full - acts).astype(jnp.bfloat16)
    scale = ROWS ** (-0.5)

    def group_grads(items):
        enc_rows, enc_shift, dec_rows = items
        pre_acts = encode(centered, enc_rows, enc_shift)
        codes = jnp.maximum(pre_acts, 0.0)
        codes_bf = codes.astype(jnp.bfloat16)
        dec_float = dec_rows.astype(jnp.float32)
        norms = jnp.sqrt(lax.optimization_barrier(jnp.sum(dec_float * dec_float, axis=1)) + 1e-06)
        back = lax.dot_general(error, dec_rows, (((1,), (1,)), ((), ())), preferred_element_type=jnp.float32)
        grad_pre = jnp.where(pre_acts > 0.0, back + sparsity_weight * norms[None, :], 0.0)
        grad_pre_bf = grad_pre.astype(jnp.bfloat16)
        data_term = lax.dot_general(codes_bf, error, (((0,), (0,)), ((), ())), preferred_element_type=jnp.float32)
        col_sums = lax.optimization_barrier(jnp.sum(codes, axis=0))
        grad_dec = scale * (data_term + sparsity_weight * col_sums[:, None] * dec_float / norms[:, None])
        grad_enc = scale * lax.dot_general(grad_pre_bf, centered, (((0,), (0,)), ((), ())), preferred_element_type=jnp.float32)
        grad_bias = scale * lax.optimization_barrier(jnp.sum(grad_pre, axis=0))
        return (grad_enc, grad_dec, grad_bias)
    grad_enc, grad_dec, grad_bias = lax.map(group_grads, (enc_groups, bias_groups, dec_groups))
    return (recon, grad_enc.reshape(LATENTS, D), grad_dec.reshape(LATENTS, D), grad_bias.reshape(LATENTS))
```

```python
import jax
import jax.numpy as jnp
from jax import lax
from jax.experimental import pallas as pl
from jax.experimental.pallas import tpu as pltpu
from jax.sharding import Mesh
from jax.sharding import PartitionSpec as P


AXES = ("zl", "c", "y", "x", "h")
MESH = pl.DeviceIdType.MESH
F32, BF16 = jnp.float32, jnp.bfloat16
SPARSITY = 0.5
NZ, SIDE, ROWS, D, OWN, LAT = 8, 4, 256, 2048, 16, 256
PORTION = ROWS // 2
SUB = PORTION // 2
CH = SUB // 2
WE = D + 128
GE = D + 256
TILE = 512


class Semaphores:
    def __init__(self):
        self.names = {}

    def __call__(self, *name):
        return self.names.setdefault(name, len(self.names))


N_SEMS = 128
NT = (((1,), (1,)), ((), ()))


def kernel(
    acts, dbias, encb, dec, recon, genc, gdec, gbias,
    cent, wenc, wdec, codes, codes_t, pown, psend, precv, psum, rsp, rsm, err, acc_e, acc_d, gb, cs,
    pay_e, pay_d, e_far, e_near, tot_e, e_last, d_far, d_near, tot_d, d_last, rec, ssem, rsem,
):
    zl, c, y, x, h = [lax.axis_index(a) for a in AXES]
    z = 2 * h + zl
    sems = Semaphores()
    pending = []

    def wrap(v, n):
        return lax.rem(v + 2 * n, n)

    def at_z(dz):
        q = wrap(z + dz, NZ)
        return (lax.rem(q, 2), c, y, x, lax.div(q, 2))

    def at_y(dy):
        return (zl, c, wrap(y + dy, SIDE), x, h)

    def at_x(dx):
        return (zl, c, y, wrap(x + dx, SIDE), h)

    partner = (zl, 1 - c, y, x, h)
    pair = (1 - zl, c, y, x, h)

    def copy(src, dst, sem, dev):
        return pltpu.make_async_remote_copy(
            src_ref=src, dst_ref=dst, send_sem=ssem.at[sem], recv_sem=rsem.at[sem], device_id=dev, device_id_type=MESH
        )

    def send(src, dst, sem, dev):
        cp = copy(src, dst, sem, dev)
        cp.start()
        pending.append(cp)

    def arrive(dst, sem):
        copy(dst, dst, sem, partner).wait_recv()

    def rows(ref, p, k, core=None):
        who = c if core is None else core
        return ref.at[p, pl.ds(pl.multiple_of(who * SUB + k * CH, CH), CH)]

    barrier = pltpu.get_barrier_semaphore()
    friends = [partner, at_z(1), at_z(-1)] + [at_y(d) for d in (1, 2, 3)] + [at_x(d) for d in (1, 2, 3)]
    for f in friends:
        pl.semaphore_signal(barrier, inc=1, device_id=f, device_id_type=MESH)
    pl.semaphore_wait(barrier, len(friends))

    for d in (1, 2, 3):
        send(encb, wenc.at[y, x], sems("we1", d), at_x(d))
        send(dec, wdec.at[y, x], sems("wd1", d), at_y(d))

    for q in range(2):
        cent[2 * h + q] = (acts[q * PORTION : (q + 1) * PORTION] - dbias[...]).astype(BF16)
    up = [wrap(2 * h + o, NZ) for o in (-2, -1, -4)]
    down = [wrap(2 * h + o, NZ) for o in (3, 2, 5)]
    for j in range(3):
        for k in range(2):
            sems("ap", j, k), sems("am", j, k)

    def piece(p, k):
        return rows(cent, p, k)

    for j in range(2):
        for k in range(2):
            @pl.when(zl == 1)
            def _(j=j, k=k):
                copy(piece(2 * h + j, k), piece(2 * h + j, k), sems("ap", j, k), at_z(1)).start()

            @pl.when(zl == 0)
            def _(j=j, k=k):
                copy(piece(2 * h + 1 - j, k), piece(2 * h + 1 - j, k), sems("am", j, k), at_z(-1)).start()

    wenc[y, x] = encb[...]
    wdec[y, x] = dec[...]

    def relay_acts(j, k):
        for name, at, dz, first in (("ap", up, 1, 0), ("am", down, -1, 1)):
            part = piece(at[j], k)
            arrive(part, sems(name, j, k))

            @pl.when(zl == first)
            def _():
                copy(part, part, sems(name, j, k), at_z(dz)).start()

            if j == 0:
                @pl.when(zl != first)
                def _():
                    copy(part, part, sems(name, 2, k), at_z(dz)).start()

            send(part, part, sems(name + "c", j, k), partner)

    def from_partner(j):
        for name, at in (("ap", up), ("am", down)):
            for k in range(2):
                arrive(rows(cent, at[j], k, 1 - c), sems(name + "c", j, k))

    relay_acts(0, 0)
    for d in (1, 2, 3):
        arrive(wenc.at[y, wrap(x - d, SIDE)], sems("we1", d))
        arrive(wdec.at[wrap(y - d, SIDE), x], sems("wd1", d))
    for s in (1, -1):
        send(wenc.at[y], wenc.at[y], sems("we2", s), at_y(s))
        send(wdec.at[:, x], wdec.at[:, x], sems("wd2", s), at_x(s))
    relay_acts(0, 1)
    relay_acts(1, 0)
    for s in (1, -1):
        half = pl.ds(0 if s == 1 else 2, 2)
        yn, xn = wrap(y - s, SIDE), wrap(x - s, SIDE)
        arrive(wenc.at[yn], sems("we2", s))
        send(wenc.at[yn, half], wenc.at[yn, half], sems("we3", s), at_y(s))
        arrive(wdec.at[:, xn], sems("wd2", s))
        send(wdec.at[half, xn], wdec.at[half, xn], sems("wd3", s), at_x(s))
    relay_acts(1, 1)
    relay_acts(2, 0)
    for s in (1, -1):
        half = pl.ds(0 if s == 1 else 2, 2)
        arrive(wenc.at[wrap(y + 2, SIDE), half], sems("we3", s))
        arrive(wdec.at[half, wrap(x + 2, SIDE)], sems("wd3", s))

    def encode(b):
        block = cent[pl.ds(2 * b, 2)].reshape(ROWS, D)
        weights = wenc[:, :, :, :D].reshape(LAT, D)
        shift = wenc[:, :, :, D:].reshape(LAT, 128).astype(F32)
        pre = lax.dot_general(weights, block, NT, preferred_element_type=F32)
        value = jnp.maximum(pre + jnp.concatenate([shift, shift], axis=1), 0.0)
        turned = value.T.astype(BF16)
        for q in range(2):
            for who in range(2):
                codes[b, who, q * SUB : (q + 1) * SUB] = turned[q * PORTION + who * SUB : q * PORTION + (who + 1) * SUB]
        codes_t[b] = value.astype(BF16)
        return value[:, :128] + value[:, 128:]

    def decode(b, order):
        for t in range(0, D, TILE):
            right = wdec[:, :, :, t : t + TILE].reshape(LAT, TILE)
            other = jnp.dot(codes[b, 1 - c], right, preferred_element_type=F32).astype(BF16)
            mine = jnp.dot(codes[b, c], right, preferred_element_type=F32)
            for q in range(2):
                psend[2 * b + q, :, t : t + TILE] = other[q * SUB : (q + 1) * SUB]
                pown[2 * b + q, :, t : t + TILE] = mine[q * SUB : (q + 1) * SUB]
        for q in range(2):
            send(psend.at[2 * b + q], precv.at[2 * b + q], sems("px", order, q), partner)

    near = 1 - 2 * zl
    blocks = [h, wrap(h - near, SIDE), wrap(h + near, SIDE), wrap(h + 2, SIDE)]
    cs[...] = encode(blocks[0])
    relay_acts(2, 1)
    decode(blocks[0], 0)
    from_partner(0)
    from_partner(1)
    for i in (1, 2):
        cs[...] += encode(blocks[i])
        decode(blocks[i], i)
    from_partner(2)
    cs[...] += encode(blocks[3])
    decode(blocks[3], 3)

    for i in range(4):
        for q in range(2):
            arrive(precv.at[2 * blocks[i] + q], sems("px", i, q))

    def part_sum(p, k):
        r = slice(k * CH, (k + 1) * CH)
        return pown[p, r] + precv[p, r].astype(F32)

    def pass_on(s, sign, k, with_recv):
        buf, name = (rsp, "rp") if sign == 1 else (rsm, "rm")
        r = slice(k * CH, (k + 1) * CH)
        p = wrap(z + sign * (4 - s), NZ)
        total = part_sum(p, k)
        if with_recv:
            arrive(buf.at[s - 1, r], sems(name, s - 1, k))
            total = total + buf[s - 1, r].astype(F32)
        psum[p, r] = total.astype(BF16)
        send(psum.at[p, r], buf.at[s, r], sems(name, s, k), at_z(sign))

    pass_on(0, 1, 0, False)
    pass_on(0, -1, 1, False)
    pass_on(1, 1, 1, False)
    pass_on(1, -1, 0, False)
    pass_on(1, 1, 0, True)
    pass_on(1, -1, 1, True)
    for s in (2, 3):
        for k in range(2):
            pass_on(s, 1, 1 - k, True)
            pass_on(s, -1, k, True)

    norms = []
    for q in range(2):
        rows_q = wdec[2 * q : 2 * q + 2].reshape(LAT // 2, D).astype(F32)
        norms.append(jnp.sqrt(jnp.sum(rows_q * rows_q, axis=1, keepdims=True) + 1e-06))
    norms = jnp.concatenate(norms, axis=0)

    own_rows = zl * PORTION + c * SUB
    for k in range(2):
        r = slice(k * CH, (k + 1) * CH)
        here = pl.ds(pl.multiple_of(own_rows + k * CH, CH), CH)
        total = part_sum(z, k)
        arrive(rsp.at[3, r], sems("rp", 3, k))
        arrive(rsm.at[3, r], sems("rm", 3, k))
        full = total + rsp[3, r].astype(F32) + rsm[3, r].astype(F32) + dbias[...]
        rec[here] = full.astype(BF16)
        err[z, pl.ds(pl.multiple_of(c * SUB + k * CH, CH), CH)] = (full - acts[here]).astype(BF16)
        mine = rows(err, z, k)
        send(mine, mine, sems("gp", 0, k), at_z(1))
        send(mine, mine, sems("gm", 0, k), at_z(-1))
        send(mine, mine, sems("go", k), partner)

    def relay_err(s):
        for k in range(2):
            for sign, name in ((1, "gp"), (-1, "gm")):
                kept = 0 if sign == 1 else 1
                if s == 3 and k != kept:
                    continue
                part = rows(err, wrap(z - sign * (s + 1), NZ), k)
                arrive(part, sems(name, s, k))
                if s < 2 or (s == 2 and k == kept):
                    send(part, part, sems(name, s + 1, k), at_z(sign))
                send(part, part, sems(name + "c", s, k), partner)

    def err_from_partner(s):
        for k in range(2):
            for sign, name in ((1, "gp"), (-1, "gm")):
                kept = 0 if sign == 1 else 1
                if s == 3 and k != kept:
                    continue
                arrive(rows(err, wrap(z - sign * (s + 1), NZ), k, 1 - c), sems(name + "c", s, k))

    def backward(b, first, last):
        block = err[pl.ds(2 * b, 2)].reshape(ROWS, D)
        weights = wdec[...].reshape(LAT, D)
        back = lax.dot_general(weights, block, NT, preferred_element_type=F32)
        kept = codes_t[b]
        grad_pre = jnp.where(kept.astype(F32) > 0.0, back + SPARSITY * norms, 0.0)
        folded = grad_pre[:, :128] + grad_pre[:, 128:]
        gb[...] = folded if first else gb[...] + folded
        grad_bf = grad_pre.astype(BF16)
        for left, data, acc, pay in ((grad_bf, cent, acc_e, pay_e), (kept, err, acc_d, pay_d)):
            for t in range(0, D, TILE):
                right = data[pl.ds(2 * b, 2), :, t : t + TILE].reshape(ROWS, TILE)
                total = jnp.dot(left, right, preferred_element_type=F32)
                if not first:
                    total = total + acc[:, t : t + TILE]
                if last:
                    pay[:, :, :, t : t + TILE] = total.astype(BF16).reshape(SIDE, SIDE, OWN, TILE)
                else:
                    acc[:, t : t + TILE] = total
            if last and pay is pay_e:
                pay[:, :, :, D : D + 128] = gb[...].astype(BF16).reshape(SIDE, SIDE, OWN, 128)
                pay[:, :, :, D + 128 :] = cs[...].astype(BF16).reshape(SIDE, SIDE, OWN, 128)
            if last:
                (start_e if pay is pay_e else start_d)()

    low, high = pl.ds(0, 2), pl.ds(2, 2)

    def e_part(yy, half):
        return pay_e.at[yy, half]

    def d_part(xx, half):
        return pay_d.at[half, xx]

    def start(part, v, far, close, name, at):
        send(part(wrap(v + 2, SIDE), low), far.at[0], sems(name, "far", 1), at(1))
        send(part(wrap(v + 2, SIDE), high), far.at[1], sems(name, "far", -1), at(-1))
        send(part(wrap(v + 1, SIDE), high), close.at[0, high], sems(name, "own", 1), at(1))
        send(part(wrap(v - 1, SIDE), low), close.at[1, low], sems(name, "own", -1), at(-1))

    def start_e():
        start(e_part, y, e_far, e_near, "e", at_y)

    def start_d():
        start(d_part, x, d_far, d_near, "d", at_x)

    def forward_sum(part, v, far, close, name, at):
        for i, s, half in ((0, 1, low), (1, -1, high)):
            arrive(far.at[i], sems(name, "far", s))
            block = part(wrap(v + s, SIDE), half)
            block[...] = (block[...].astype(F32) + far[i].astype(F32)).astype(BF16)
            send(block, close.at[i, half], sems(name, "sum", s), at(s))

    def at_owner(part, v, w, close, tot, last, name, at):
        for i, s, summed, plain in ((0, 1, low, high), (1, -1, high, low)):
            arrive(close.at[i, plain], sems(name, "own", s))
            arrive(close.at[i, summed], sems(name, "sum", s))
        tot[...] = (
            part(v, pl.ds(0, SIDE))[...].astype(F32) + close[0].astype(F32) + close[1].astype(F32)
        ).astype(BF16)
        for d in (1, 2, 3):
            send(tot.at[wrap(w + d, SIDE)], last.at[d - 1], sems(name, "last", d), at(d))

    def owned(w, tot, last, name):
        total = tot[w].astype(F32)
        for d in (1, 2, 3):
            arrive(last.at[d - 1], sems(name, "last", d))
            total = total + last[d - 1].astype(F32)
        return total

    relay_err(0)
    for k in range(2):
        arrive(rows(err, z, k, 1 - c), sems("go", k))
    err_from_partner(0)
    backward(blocks[0], True, False)
    relay_err(1)
    err_from_partner(1)
    backward(blocks[1], False, False)
    relay_err(2)
    err_from_partner(2)
    backward(blocks[2], False, False)
    relay_err(3)
    own_rec = rec.at[pl.ds(pl.multiple_of(own_rows, SUB), SUB)]
    send(own_rec, own_rec, sems("ro"), partner)
    send(own_rec, own_rec, sems("rz"), pair)
    err_from_partner(3)
    backward(blocks[3], False, True)

    forward_sum(e_part, y, e_far, e_near, "e", at_y)
    forward_sum(d_part, x, d_far, d_near, "d", at_x)
    pair_rec = rec.at[pl.ds(pl.multiple_of((1 - zl) * PORTION + c * SUB, SUB), SUB)]
    arrive(pair_rec, sems("rz"))
    send(pair_rec, pair_rec, sems("rzc"), partner)
    at_owner(e_part, y, x, e_near, tot_e, e_last, "e", at_x)
    at_owner(d_part, x, y, d_near, tot_d, d_last, "d", at_y)
    arrive(rec.at[pl.ds(pl.multiple_of(zl * PORTION + (1 - c) * SUB, SUB), SUB)], sems("ro"))
    arrive(rec.at[pl.ds(pl.multiple_of((1 - zl) * PORTION + (1 - c) * SUB, SUB), SUB)], sems("rzc"))
    recon[...] = rec[...]

    scale = (ROWS * SIDE * SIDE * SIDE) ** -0.5
    total = owned(x, tot_e, e_last, "e")
    genc[...] = scale * total[:, :D]
    gbias[...] = jnp.broadcast_to(scale * jnp.sum(total[:, D : D + 128], axis=1, keepdims=True), (OWN, 128))
    col_sums = jnp.sum(total[:, D + 128 :], axis=1, keepdims=True)
    mine = dec[...].astype(F32)
    own_norms = jnp.sqrt(jnp.sum(mine * mine, axis=1, keepdims=True) + 1e-06)
    total = owned(y, tot_d, d_last, "d")
    gdec[...] = scale * (total + SPARSITY * col_sums * mine / own_norms)

    for name, at, dz in (("ap", up, 1), ("am", down, -1)):
        for j in range(3):
            for k in range(2):
                copy(piece(at[j], k), piece(at[j], k), sems(name, j, k), at_z(dz)).wait_send()
    for cp in pending:
        cp.wait_send()


def per_device(acts, dec_bias, enc_weight, enc_bias, dec_weight):
    encb = jnp.concatenate([enc_weight, jnp.broadcast_to(enc_bias[:, None], (OWN, 128))], axis=1)
    vmem = pl.BlockSpec(memory_space=pltpu.VMEM)
    recon, genc, gdec, gbias = pl.pallas_call(
        kernel,
        name="step",
        out_shape=(
            jax.ShapeDtypeStruct((ROWS, D), BF16),
            jax.ShapeDtypeStruct((OWN, D), F32),
            jax.ShapeDtypeStruct((OWN, D), F32),
            jax.ShapeDtypeStruct((OWN, 128), F32),
        ),
        in_specs=[vmem] * 4,
        out_specs=(vmem,) * 4,
        scratch_shapes=[
            pltpu.VMEM((NZ, PORTION, D), BF16),
            pltpu.VMEM((SIDE, SIDE, OWN, WE), BF16),
            pltpu.VMEM((SIDE, SIDE, OWN, D), BF16),
            pltpu.VMEM((SIDE, 2, PORTION, LAT), BF16),
            pltpu.VMEM((SIDE, LAT, ROWS), BF16),
            pltpu.VMEM((NZ, SUB, D), F32),
            pltpu.VMEM((NZ, SUB, D), BF16),
            pltpu.VMEM((NZ, SUB, D), BF16),
            pltpu.VMEM((NZ, SUB, D), BF16),
            pltpu.VMEM((4, SUB, D), BF16),
            pltpu.VMEM((4, SUB, D), BF16),
            pltpu.VMEM((NZ, PORTION, D), BF16),
            pltpu.VMEM((LAT, D), F32),
            pltpu.VMEM((LAT, D), F32),
            pltpu.VMEM((LAT, 128), F32),
            pltpu.VMEM((LAT, 128), F32),
            pltpu.VMEM((SIDE, SIDE, OWN, GE), BF16),
            pltpu.VMEM((SIDE, SIDE, OWN, D), BF16),
            pltpu.VMEM((2, 2, OWN, GE), BF16),
            pltpu.VMEM((2, SIDE, OWN, GE), BF16),
            pltpu.VMEM((SIDE, OWN, GE), BF16),
            pltpu.VMEM((3, OWN, GE), BF16),
            pltpu.VMEM((2, 2, OWN, D), BF16),
            pltpu.VMEM((2, SIDE, OWN, D), BF16),
            pltpu.VMEM((SIDE, OWN, D), BF16),
            pltpu.VMEM((3, OWN, D), BF16),
            pltpu.VMEM((ROWS, D), BF16),
            pltpu.SemaphoreType.DMA((N_SEMS,)),
            pltpu.SemaphoreType.DMA((N_SEMS,)),
        ],
        compiler_params=pltpu.CompilerParams(collective_id=0, has_side_effects=True, vmem_limit_bytes=60 << 20),
    )(acts, dec_bias[None, :], encb, dec_weight)
    return recon, genc, gdec, gbias[:, 0]


def solution(mesh):
    torus = Mesh(mesh.devices.reshape(2, 2, SIDE, SIDE, SIDE), AXES)
    wide = P(("y", "x", "h"), None)
    return jax.shard_map(
        per_device,
        mesh=torus,
        in_specs=(wide, P(), P(AXES, None), P(AXES), P(AXES, None)),
        out_specs=(wide, P(AXES, None), P(AXES, None), P(AXES)),
        check_vma=False,
    )
```

```python
import jax
import jax.numpy as jnp
from jax import lax
from jax.experimental import pallas as pl
from jax.experimental.pallas import tpu as pltpu
from jax.sharding import Mesh
from jax.sharding import PartitionSpec as P


AXES = ("zl", "c", "y", "x", "h")
MESH = pl.DeviceIdType.MESH
F32, BF16 = jnp.float32, jnp.bfloat16
SPARSITY = 0.5
NZ, SIDE, ROWS, D, OWN, LAT = 8, 4, 256, 2048, 16, 256
PORTION = ROWS // 2
SUB = PORTION // 2
CH = SUB // 2
WE = D + 128
GE = D + 256
TILE = 512


class Semaphores:
    def __init__(self):
        self.names = {}

    def __call__(self, *name):
        return self.names.setdefault(name, len(self.names))


N_SEMS = 128
NT = (((1,), (1,)), ((), ()))


def kernel(
    acts, dbias, enc, bias, dec, recon, genc, gdec, gbias,
    cent, wenc, wdec, codes, codes_t, pown, psend, precv, psum, rsp, rsm, err, acc_e, acc_d, gb, cs,
    pay_e, pay_d, e_far, e_near, tot_e, e_last, d_far, d_near, tot_d, d_last, rec, ssem, rsem,
):
    zl, c, y, x, h = [lax.axis_index(a) for a in AXES]
    z = 2 * h + zl
    sems = Semaphores()
    pending = []

    def wrap(v, n):
        return lax.rem(v + 2 * n, n)

    def at_z(dz):
        q = wrap(z + dz, NZ)
        return (lax.rem(q, 2), c, y, x, lax.div(q, 2))

    def at_y(dy):
        return (zl, c, wrap(y + dy, SIDE), x, h)

    def at_x(dx):
        return (zl, c, y, wrap(x + dx, SIDE), h)

    partner = (zl, 1 - c, y, x, h)
    pair = (1 - zl, c, y, x, h)

    def copy(src, dst, sem, dev):
        return pltpu.make_async_remote_copy(
            src_ref=src, dst_ref=dst, send_sem=ssem.at[sem], recv_sem=rsem.at[sem], device_id=dev, device_id_type=MESH
        )

    def send(src, dst, sem, dev):
        cp = copy(src, dst, sem, dev)
        cp.start()
        pending.append(cp)

    def arrive(dst, sem):
        copy(dst, dst, sem, partner).wait_recv()

    def rows(ref, p, k, core=None):
        who = c if core is None else core
        return ref.at[p, pl.ds(pl.multiple_of(who * SUB + k * CH, CH), CH)]

    barrier = pltpu.get_barrier_semaphore()
    friends = [partner, at_z(1), at_z(-1)] + [at_y(d) for d in (1, 2, 3)] + [at_x(d) for d in (1, 2, 3)]
    for f in friends:
        pl.semaphore_signal(barrier, inc=1, device_id=f, device_id_type=MESH)
    pl.semaphore_wait(barrier, len(friends))

    eye = lax.broadcasted_iota(jnp.int32, (OWN, OWN), 0) == lax.broadcasted_iota(jnp.int32, (OWN, OWN), 1)
    column = jnp.sum(jnp.where(eye, bias[...].astype(F32), 0.0), axis=1, keepdims=True)
    wenc[y, x, :, :D] = enc[...]
    wenc[y, x, :, D:] = jnp.broadcast_to(column, (OWN, 128)).astype(BF16)
    wdec[y, x] = dec[...]
    for d in (1, 2, 3):
        send(wenc.at[y, x], wenc.at[y, x], sems("we1", d), at_x(d))
        send(dec, wdec.at[y, x], sems("wd1", d), at_y(d))

    for q in range(2):
        cent[2 * h + q] = (acts[q * PORTION : (q + 1) * PORTION] - dbias[...]).astype(BF16)
    def mirrored(even, odd):
        return wrap(2 * h + even + zl * (odd - even), NZ)

    coming = {
        "a": [mirrored(-2, 3), mirrored(-1, 2), mirrored(-4, 5)],
        "b": [mirrored(3, -2), mirrored(2, -1), mirrored(5, -4)],
    }
    outer = at_z(2 * zl - 1)

    def piece(p, k):
        return rows(cent, p, k)

    for j in range(2):
        for k in range(2):
            part = piece(mirrored(1 - j, j), k)
            send(part, part, sems("a", j, k), outer)

    def relay_acts(name, j, k):
        part = piece(coming[name][j], k)
        arrive(part, sems(name, j, k))
        if name == "a":
            send(part, part, sems("b", j, k), pair)
        elif j == 0:
            send(part, part, sems("a", 2, k), outer)
        send(part, part, sems(name + "c", j, k), partner)

    def from_partner(name, js):
        for j in js:
            for k in range(2):
                arrive(rows(cent, coming[name][j], k, 1 - c), sems(name + "c", j, k))

    relay_acts("a", 0, 0)
    for d in (1, 2, 3):
        arrive(wenc.at[y, wrap(x - d, SIDE)], sems("we1", d))
        arrive(wdec.at[wrap(y - d, SIDE), x], sems("wd1", d))
    for s in (1, -1):
        send(wenc.at[y], wenc.at[y], sems("we2", s), at_y(s))
        send(wdec.at[:, x], wdec.at[:, x], sems("wd2", s), at_x(s))
    relay_acts("a", 0, 1)
    relay_acts("b", 0, 0)
    relay_acts("a", 1, 0)
    relay_acts("b", 0, 1)
    for s in (1, -1):
        half = pl.ds(0 if s == 1 else 2, 2)
        yn, xn = wrap(y - s, SIDE), wrap(x - s, SIDE)
        arrive(wenc.at[yn], sems("we2", s))
        send(wenc.at[yn, half], wenc.at[yn, half], sems("we3", s), at_y(s))
        arrive(wdec.at[:, xn], sems("wd2", s))
        send(wdec.at[half, xn], wdec.at[half, xn], sems("wd3", s), at_x(s))
    relay_acts("a", 1, 1)
    relay_acts("b", 1, 0)
    relay_acts("a", 2, 0)
    for s in (1, -1):
        half = pl.ds(0 if s == 1 else 2, 2)
        arrive(wenc.at[wrap(y + 2, SIDE), half], sems("we3", s))
        arrive(wdec.at[half, wrap(x + 2, SIDE)], sems("wd3", s))

    def encode(b):
        block = cent[pl.ds(2 * b, 2)].reshape(ROWS, D)
        weights = wenc[:, :, :, :D].reshape(LAT, D)
        shift = wenc[:, :, :, D:].reshape(LAT, 128).astype(F32)
        pre = lax.dot_general(weights, block, NT, preferred_element_type=F32)
        value = jnp.maximum(pre + jnp.concatenate([shift, shift], axis=1), 0.0)
        turned = value.T.astype(BF16)
        for q in range(2):
            for who in range(2):
                codes[b, who, q * SUB : (q + 1) * SUB] = turned[q * PORTION + who * SUB : q * PORTION + (who + 1) * SUB]
        codes_t[b] = value.astype(BF16)
        return value[:, :128] + value[:, 128:]

    def decode(b, order):
        for t in range(0, D, TILE):
            right = wdec[:, :, :, t : t + TILE].reshape(LAT, TILE)
            other = jnp.dot(codes[b, 1 - c], right, preferred_element_type=F32).astype(BF16)
            mine = jnp.dot(codes[b, c], right, preferred_element_type=F32)
            for q in range(2):
                psend[2 * b + q, :, t : t + TILE] = other[q * SUB : (q + 1) * SUB]
                pown[2 * b + q, :, t : t + TILE] = mine[q * SUB : (q + 1) * SUB]
        for q in range(2):
            send(psend.at[2 * b + q], precv.at[2 * b + q], sems("px", order, q), partner)

    near = 1 - 2 * zl
    blocks = [h, wrap(h - near, SIDE), wrap(h + near, SIDE), wrap(h + 2, SIDE)]
    relay_acts("b", 1, 1)
    cs[...] = encode(blocks[0])
    relay_acts("a", 2, 1)
    decode(blocks[0], 0)
    relay_acts("b", 2, 0)
    from_partner("a", (0, 1))
    cs[...] += encode(blocks[1])
    decode(blocks[1], 1)
    relay_acts("b", 2, 1)
    from_partner("b", (0, 1))
    cs[...] += encode(blocks[2])
    decode(blocks[2], 2)
    from_partner("a", (2,))
    from_partner("b", (2,))
    cs[...] += encode(blocks[3])
    decode(blocks[3], 3)

    for i in range(4):
        for q in range(2):
            arrive(precv.at[2 * blocks[i] + q], sems("px", i, q))

    def part_sum(p, k):
        r = slice(k * CH, (k + 1) * CH)
        return pown[p, r] + precv[p, r].astype(F32)

    def pass_on(s, sign, k, with_recv):
        buf, name = (rsp, "rp") if sign == 1 else (rsm, "rm")
        r = slice(k * CH, (k + 1) * CH)
        p = wrap(z + sign * (4 - s), NZ)
        total = part_sum(p, k)
        if with_recv:
            arrive(buf.at[s - 1, r], sems(name, s - 1, k))
            total = total + buf[s - 1, r].astype(F32)
        psum[p, r] = total.astype(BF16)
        send(psum.at[p, r], buf.at[s, r], sems(name, s, k), at_z(sign))

    pass_on(0, 1, 0, False)
    pass_on(0, -1, 1, False)
    pass_on(1, 1, 1, False)
    pass_on(1, -1, 0, False)
    pass_on(1, 1, 0, True)
    pass_on(1, -1, 1, True)
    for s in (2, 3):
        for k in range(2):
            pass_on(s, 1, 1 - k, True)
            pass_on(s, -1, k, True)

    norms = []
    for q in range(2):
        rows_q = wdec[2 * q : 2 * q + 2].reshape(LAT // 2, D).astype(F32)
        norms.append(jnp.sqrt(jnp.sum(rows_q * rows_q, axis=1, keepdims=True) + 1e-06))
    norms = jnp.concatenate(norms, axis=0)

    own_rows = zl * PORTION + c * SUB
    for k in range(2):
        r = slice(k * CH, (k + 1) * CH)
        here = pl.ds(pl.multiple_of(own_rows + k * CH, CH), CH)
        total = part_sum(z, k)
        arrive(rsp.at[3, r], sems("rp", 3, k))
        arrive(rsm.at[3, r], sems("rm", 3, k))
        full = total + rsp[3, r].astype(F32) + rsm[3, r].astype(F32) + dbias[...]
        rec[here] = full.astype(BF16)
        err[z, pl.ds(pl.multiple_of(c * SUB + k * CH, CH), CH)] = (full - acts[here]).astype(BF16)
        mine = rows(err, z, k)
        send(mine, mine, sems("gp", 0, k), at_z(1))
        send(mine, mine, sems("gm", 0, k), at_z(-1))
        send(mine, mine, sems("go", k), partner)

    def relay_err(s):
        for k in range(2):
            for sign, name in ((1, "gp"), (-1, "gm")):
                kept = 0 if sign == 1 else 1
                if s == 3 and k != kept:
                    continue
                part = rows(err, wrap(z - sign * (s + 1), NZ), k)
                arrive(part, sems(name, s, k))
                if s < 2 or (s == 2 and k == kept):
                    send(part, part, sems(name, s + 1, k), at_z(sign))
                send(part, part, sems(name + "c", s, k), partner)

    def err_from_partner(s):
        for k in range(2):
            for sign, name in ((1, "gp"), (-1, "gm")):
                kept = 0 if sign == 1 else 1
                if s == 3 and k != kept:
                    continue
                arrive(rows(err, wrap(z - sign * (s + 1), NZ), k, 1 - c), sems(name + "c", s, k))

    def backward(b, first, last):
        block = err[pl.ds(2 * b, 2)].reshape(ROWS, D)
        weights = wdec[...].reshape(LAT, D)
        back = lax.dot_general(weights, block, NT, preferred_element_type=F32)
        kept = codes_t[b]
        grad_pre = jnp.where(kept.astype(F32) > 0.0, back + SPARSITY * norms, 0.0)
        folded = grad_pre[:, :128] + grad_pre[:, 128:]
        gb[...] = folded if first else gb[...] + folded
        grad_bf = grad_pre.astype(BF16)
        for left, data, acc, pay in ((grad_bf, cent, acc_e, pay_e), (kept, err, acc_d, pay_d)):
            for t in range(0, D, TILE):
                right = data[pl.ds(2 * b, 2), :, t : t + TILE].reshape(ROWS, TILE)
                total = jnp.dot(left, right, preferred_element_type=F32)
                if not first:
                    total = total + acc[:, t : t + TILE]
                if last:
                    pay[:, :, :, t : t + TILE] = total.astype(BF16).reshape(SIDE, SIDE, OWN, TILE)
                else:
                    acc[:, t : t + TILE] = total
            if last and pay is pay_e:
                pay[:, :, :, D : D + 128] = gb[...].astype(BF16).reshape(SIDE, SIDE, OWN, 128)
                pay[:, :, :, D + 128 :] = cs[...].astype(BF16).reshape(SIDE, SIDE, OWN, 128)
            if last:
                (start_e if pay is pay_e else start_d)()

    low, high = pl.ds(0, 2), pl.ds(2, 2)

    def e_part(yy, half):
        return pay_e.at[yy, half]

    def d_part(xx, half):
        return pay_d.at[half, xx]

    def start(part, v, far, close, name, at):
        send(part(wrap(v + 2, SIDE), low), far.at[0], sems(name, "far", 1), at(1))
        send(part(wrap(v + 2, SIDE), high), far.at[1], sems(name, "far", -1), at(-1))
        send(part(wrap(v + 1, SIDE), high), close.at[0, high], sems(name, "own", 1), at(1))
        send(part(wrap(v - 1, SIDE), low), close.at[1, low], sems(name, "own", -1), at(-1))

    def start_e():
        start(e_part, y, e_far, e_near, "e", at_y)

    def start_d():
        start(d_part, x, d_far, d_near, "d", at_x)

    def forward_sum(part, v, far, close, name, at):
        for i, s, half in ((0, 1, low), (1, -1, high)):
            arrive(far.at[i], sems(name, "far", s))
            block = part(wrap(v + s, SIDE), half)
            block[...] = (block[...].astype(F32) + far[i].astype(F32)).astype(BF16)
            send(block, close.at[i, half], sems(name, "sum", s), at(s))

    def at_owner(part, v, w, close, tot, last, name, at):
        for i, s, summed, plain in ((0, 1, low, high), (1, -1, high, low)):
            arrive(close.at[i, plain], sems(name, "own", s))
            arrive(close.at[i, summed], sems(name, "sum", s))
        tot[...] = (
            part(v, pl.ds(0, SIDE))[...].astype(F32) + close[0].astype(F32) + close[1].astype(F32)
        ).astype(BF16)
        for d in (1, 2, 3):
            send(tot.at[wrap(w + d, SIDE)], last.at[d - 1], sems(name, "last", d), at(d))

    def owned(w, tot, last, name):
        total = tot[w].astype(F32)
        for d in (1, 2, 3):
            arrive(last.at[d - 1], sems(name, "last", d))
            total = total + last[d - 1].astype(F32)
        return total

    relay_err(0)
    for k in range(2):
        arrive(rows(err, z, k, 1 - c), sems("go", k))
    err_from_partner(0)
    backward(blocks[0], True, False)
    relay_err(1)
    err_from_partner(1)
    backward(blocks[1], False, False)
    relay_err(2)
    err_from_partner(2)
    backward(blocks[2], False, False)
    relay_err(3)
    own_rec = rec.at[pl.ds(pl.multiple_of(own_rows, SUB), SUB)]
    send(own_rec, own_rec, sems("ro"), partner)
    send(own_rec, own_rec, sems("rz"), pair)
    err_from_partner(3)
    backward(blocks[3], False, True)

    forward_sum(e_part, y, e_far, e_near, "e", at_y)
    forward_sum(d_part, x, d_far, d_near, "d", at_x)
    pair_rec = rec.at[pl.ds(pl.multiple_of((1 - zl) * PORTION + c * SUB, SUB), SUB)]
    arrive(pair_rec, sems("rz"))
    send(pair_rec, pair_rec, sems("rzc"), partner)
    at_owner(e_part, y, x, e_near, tot_e, e_last, "e", at_x)
    at_owner(d_part, x, y, d_near, tot_d, d_last, "d", at_y)
    arrive(rec.at[pl.ds(pl.multiple_of(zl * PORTION + (1 - c) * SUB, SUB), SUB)], sems("ro"))
    arrive(rec.at[pl.ds(pl.multiple_of((1 - zl) * PORTION + (1 - c) * SUB, SUB), SUB)], sems("rzc"))
    recon[...] = rec[...]

    scale = (ROWS * SIDE * SIDE * SIDE) ** -0.5
    total = owned(x, tot_e, e_last, "e")
    genc[...] = scale * total[:, :D]
    gbias[...] = jnp.broadcast_to(scale * jnp.sum(total[:, D : D + 128], axis=1, keepdims=True), (OWN, 128))
    col_sums = jnp.sum(total[:, D + 128 :], axis=1, keepdims=True)
    mine = dec[...].astype(F32)
    own_norms = jnp.sqrt(jnp.sum(mine * mine, axis=1, keepdims=True) + 1e-06)
    total = owned(y, tot_d, d_last, "d")
    gdec[...] = scale * (total + SPARSITY * col_sums * mine / own_norms)

    for cp in pending:
        cp.wait_send()


def per_device(acts, dec_bias, enc_weight, enc_bias, dec_weight):
    vmem = pl.BlockSpec(memory_space=pltpu.VMEM)
    recon, genc, gdec, gbias = pl.pallas_call(
        kernel,
        name="step",
        out_shape=(
            jax.ShapeDtypeStruct((ROWS, D), BF16),
            jax.ShapeDtypeStruct((OWN, D), F32),
            jax.ShapeDtypeStruct((OWN, D), F32),
            jax.ShapeDtypeStruct((OWN, 128), F32),
        ),
        in_specs=[vmem] * 5,
        out_specs=(vmem,) * 4,
        scratch_shapes=[
            pltpu.VMEM((NZ, PORTION, D), BF16),
            pltpu.VMEM((SIDE, SIDE, OWN, WE), BF16),
            pltpu.VMEM((SIDE, SIDE, OWN, D), BF16),
            pltpu.VMEM((SIDE, 2, PORTION, LAT), BF16),
            pltpu.VMEM((SIDE, LAT, ROWS), BF16),
            pltpu.VMEM((NZ, SUB, D), F32),
            pltpu.VMEM((NZ, SUB, D), BF16),
            pltpu.VMEM((NZ, SUB, D), BF16),
            pltpu.VMEM((NZ, SUB, D), BF16),
            pltpu.VMEM((4, SUB, D), BF16),
            pltpu.VMEM((4, SUB, D), BF16),
            pltpu.VMEM((NZ, PORTION, D), BF16),
            pltpu.VMEM((LAT, D), F32),
            pltpu.VMEM((LAT, D), F32),
            pltpu.VMEM((LAT, 128), F32),
            pltpu.VMEM((LAT, 128), F32),
            pltpu.VMEM((SIDE, SIDE, OWN, GE), BF16),
            pltpu.VMEM((SIDE, SIDE, OWN, D), BF16),
            pltpu.VMEM((2, 2, OWN, GE), BF16),
            pltpu.VMEM((2, SIDE, OWN, GE), BF16),
            pltpu.VMEM((SIDE, OWN, GE), BF16),
            pltpu.VMEM((3, OWN, GE), BF16),
            pltpu.VMEM((2, 2, OWN, D), BF16),
            pltpu.VMEM((2, SIDE, OWN, D), BF16),
            pltpu.VMEM((SIDE, OWN, D), BF16),
            pltpu.VMEM((3, OWN, D), BF16),
            pltpu.VMEM((ROWS, D), BF16),
            pltpu.SemaphoreType.DMA((N_SEMS,)),
            pltpu.SemaphoreType.DMA((N_SEMS,)),
        ],
        compiler_params=pltpu.CompilerParams(collective_id=0, has_side_effects=True, vmem_limit_bytes=60 << 20),
    )(acts, dec_bias[None, :], enc_weight, enc_bias[None, :], dec_weight)
    return recon, genc, gdec, gbias[:, 0]


def solution(mesh):
    torus = Mesh(mesh.devices.reshape(2, 2, SIDE, SIDE, SIDE), AXES)
    wide = P(("y", "x", "h"), None)
    return jax.shard_map(
        per_device,
        mesh=torus,
        in_specs=(wide, P(), P(AXES, None), P(AXES), P(AXES, None)),
        out_specs=(wide, P(AXES, None), P(AXES, None), P(AXES)),
        check_vma=False,
    )
```

```python
import jax
import jax.numpy as jnp
from jax import lax
from jax.experimental import pallas as pl
from jax.experimental.pallas import tpu as pltpu
from jax.sharding import Mesh
from jax.sharding import PartitionSpec as P


AXES = ("zl", "c", "y", "x", "h")
MESH = pl.DeviceIdType.MESH
F32, BF16 = jnp.float32, jnp.bfloat16
SPARSITY = 0.5
NZ, SIDE, ROWS, D, OWN, LAT = 8, 4, 256, 2048, 16, 256
PORTION = ROWS // 2
SUB = PORTION // 2
CH = SUB // 2
WE = D + 128
GE = D + 256
TILE = 512


class Semaphores:
    def __init__(self):
        self.names = {}

    def __call__(self, *name):
        return self.names.setdefault(name, len(self.names))


N_SEMS = 128
NT = (((1,), (1,)), ((), ()))


def kernel(
    acts_hbm, dbias_hbm, enc_hbm, bias_hbm, dec_hbm, recon, genc, gdec, gbias, acts, dbias, bias, dec,
    cent, wenc, wdec, codes, codes_t, pown, psend, precv, psum, rsp, rsm, err, acc_e, acc_d, gb, cs,
    pay_e, pay_d, e_far, e_near, tot_e, e_last, d_far, d_near, tot_d, d_last, rec, lsem, ssem, rsem,
):
    zl, c, y, x, h = [lax.axis_index(a) for a in AXES]
    z = 2 * h + zl
    sems = Semaphores()
    pending = []

    def wrap(v, n):
        return lax.rem(v + 2 * n, n)

    def at_z(dz):
        q = wrap(z + dz, NZ)
        return (lax.rem(q, 2), c, y, x, lax.div(q, 2))

    def at_y(dy):
        return (zl, c, wrap(y + dy, SIDE), x, h)

    def at_x(dx):
        return (zl, c, y, wrap(x + dx, SIDE), h)

    partner = (zl, 1 - c, y, x, h)
    pair = (1 - zl, c, y, x, h)

    def copy(src, dst, sem, dev):
        return pltpu.make_async_remote_copy(
            src_ref=src, dst_ref=dst, send_sem=ssem.at[sem], recv_sem=rsem.at[sem], device_id=dev, device_id_type=MESH
        )

    def send(src, dst, sem, dev):
        cp = copy(src, dst, sem, dev)
        cp.start()
        pending.append(cp)

    def arrive(dst, sem):
        copy(dst, dst, sem, partner).wait_recv()

    def rows(ref, p, k, core=None):
        who = c if core is None else core
        return ref.at[p, pl.ds(pl.multiple_of(who * SUB + k * CH, CH), CH)]

    loads = [
        pltpu.make_async_copy(src, dst, lsem.at[i])
        for i, (src, dst) in enumerate(
            (
                (bias_hbm, bias),
                (enc_hbm, wenc.at[y, x, :, pl.ds(0, D)]),
                (dec_hbm, dec),
                (dbias_hbm, dbias),
                (acts_hbm, acts),
            )
        )
    ]
    for load in loads:
        load.start()
    barrier = pltpu.get_barrier_semaphore()
    friends = [partner, at_z(1), at_z(-1)] + [at_y(d) for d in (1, 2, 3)] + [at_x(d) for d in (1, 2, 3)]
    for f in friends:
        pl.semaphore_signal(barrier, inc=1, device_id=f, device_id_type=MESH)
    for load in loads:
        load.wait()
    for q in range(2):
        cent[2 * h + q] = (acts[q * PORTION : (q + 1) * PORTION] - dbias[...]).astype(BF16)
    eye = lax.broadcasted_iota(jnp.int32, (OWN, OWN), 0) == lax.broadcasted_iota(jnp.int32, (OWN, OWN), 1)
    column = jnp.sum(jnp.where(eye, bias[...].astype(F32), 0.0), axis=1, keepdims=True)
    wenc[y, x, :, D:] = jnp.broadcast_to(column, (OWN, 128)).astype(BF16)
    wdec[y, x] = dec[...]
    pl.semaphore_wait(barrier, len(friends))

    for d in (1, 2, 3):
        send(wenc.at[y, x], wenc.at[y, x], sems("we1", d), at_x(d))
        send(dec, wdec.at[y, x], sems("wd1", d), at_y(d))

    def mirrored(even, odd):
        return wrap(2 * h + even + zl * (odd - even), NZ)

    coming = {
        "a": [mirrored(-2, 3), mirrored(-1, 2), mirrored(-4, 5)],
        "b": [mirrored(3, -2), mirrored(2, -1), mirrored(5, -4)],
    }
    outer = at_z(2 * zl - 1)

    def piece(p, k):
        return rows(cent, p, k)

    for j in range(2):
        for k in range(2):
            part = piece(mirrored(1 - j, j), k)
            send(part, part, sems("a", j, k), outer)

    def relay_acts(name, j, k):
        part = piece(coming[name][j], k)
        arrive(part, sems(name, j, k))
        if name == "a":
            send(part, part, sems("b", j, k), pair)
        elif j == 0:
            send(part, part, sems("a", 2, k), outer)
        send(part, part, sems(name + "c", j, k), partner)

    def from_partner(name, js):
        for j in js:
            for k in range(2):
                arrive(rows(cent, coming[name][j], k, 1 - c), sems(name + "c", j, k))

    relay_acts("a", 0, 0)
    for d in (1, 2, 3):
        arrive(wenc.at[y, wrap(x - d, SIDE)], sems("we1", d))
        arrive(wdec.at[wrap(y - d, SIDE), x], sems("wd1", d))
    for s in (1, -1):
        send(wenc.at[y], wenc.at[y], sems("we2", s), at_y(s))
        send(wdec.at[:, x], wdec.at[:, x], sems("wd2", s), at_x(s))
    relay_acts("a", 0, 1)
    relay_acts("b", 0, 0)
    relay_acts("a", 1, 0)
    relay_acts("b", 0, 1)
    for s in (1, -1):
        half = pl.ds(0 if s == 1 else 2, 2)
        yn, xn = wrap(y - s, SIDE), wrap(x - s, SIDE)
        arrive(wenc.at[yn], sems("we2", s))
        send(wenc.at[yn, half], wenc.at[yn, half], sems("we3", s), at_y(s))
        arrive(wdec.at[:, xn], sems("wd2", s))
        send(wdec.at[half, xn], wdec.at[half, xn], sems("wd3", s), at_x(s))
    relay_acts("a", 1, 1)
    relay_acts("b", 1, 0)
    relay_acts("a", 2, 0)
    for s in (1, -1):
        half = pl.ds(0 if s == 1 else 2, 2)
        arrive(wenc.at[wrap(y + 2, SIDE), half], sems("we3", s))
        arrive(wdec.at[half, wrap(x + 2, SIDE)], sems("wd3", s))

    def encode(b):
        block = cent[pl.ds(2 * b, 2)].reshape(ROWS, D)
        weights = wenc[:, :, :, :D].reshape(LAT, D)
        shift = wenc[:, :, :, D:].reshape(LAT, 128).astype(F32)
        pre = lax.dot_general(weights, block, NT, preferred_element_type=F32)
        value = jnp.maximum(pre + jnp.concatenate([shift, shift], axis=1), 0.0)
        turned = value.T.astype(BF16)
        for q in range(2):
            for who in range(2):
                codes[b, who, q * SUB : (q + 1) * SUB] = turned[q * PORTION + who * SUB : q * PORTION + (who + 1) * SUB]
        codes_t[b] = value.astype(BF16)
        return value[:, :128] + value[:, 128:]

    def decode(b, order):
        for t in range(0, D, TILE):
            right = wdec[:, :, :, t : t + TILE].reshape(LAT, TILE)
            other = jnp.dot(codes[b, 1 - c], right, preferred_element_type=F32).astype(BF16)
            mine = jnp.dot(codes[b, c], right, preferred_element_type=F32)
            for q in range(2):
                psend[2 * b + q, :, t : t + TILE] = other[q * SUB : (q + 1) * SUB]
                pown[2 * b + q, :, t : t + TILE] = mine[q * SUB : (q + 1) * SUB]
        for q in range(2):
            send(psend.at[2 * b + q], precv.at[2 * b + q], sems("px", order, q), partner)

    near = 1 - 2 * zl
    blocks = [h, wrap(h - near, SIDE), wrap(h + near, SIDE), wrap(h + 2, SIDE)]
    relay_acts("b", 1, 1)
    cs[...] = encode(blocks[0])
    relay_acts("a", 2, 1)
    decode(blocks[0], 0)
    relay_acts("b", 2, 0)
    from_partner("a", (0, 1))
    cs[...] += encode(blocks[1])
    decode(blocks[1], 1)
    relay_acts("b", 2, 1)
    from_partner("b", (0, 1))
    cs[...] += encode(blocks[2])
    decode(blocks[2], 2)
    from_partner("a", (2,))
    from_partner("b", (2,))
    cs[...] += encode(blocks[3])
    decode(blocks[3], 3)

    for i in range(4):
        for q in range(2):
            arrive(precv.at[2 * blocks[i] + q], sems("px", i, q))

    def part_sum(p, k):
        r = slice(k * CH, (k + 1) * CH)
        return pown[p, r] + precv[p, r].astype(F32)

    def pass_on(s, sign, k, with_recv):
        buf, name = (rsp, "rp") if sign == 1 else (rsm, "rm")
        r = slice(k * CH, (k + 1) * CH)
        p = wrap(z + sign * (4 - s), NZ)
        total = part_sum(p, k)
        if with_recv:
            arrive(buf.at[s - 1, r], sems(name, s - 1, k))
            total = total + buf[s - 1, r].astype(F32)
        psum[p, r] = total.astype(BF16)
        send(psum.at[p, r], buf.at[s, r], sems(name, s, k), at_z(sign))

    pass_on(0, 1, 0, False)
    pass_on(0, -1, 1, False)
    pass_on(1, 1, 1, False)
    pass_on(1, -1, 0, False)
    pass_on(1, 1, 0, True)
    pass_on(1, -1, 1, True)
    for s in (2, 3):
        for k in range(2):
            pass_on(s, 1, 1 - k, True)
            pass_on(s, -1, k, True)

    norms = []
    for q in range(2):
        rows_q = wdec[2 * q : 2 * q + 2].reshape(LAT // 2, D).astype(F32)
        norms.append(jnp.sqrt(jnp.sum(rows_q * rows_q, axis=1, keepdims=True) + 1e-06))
    norms = jnp.concatenate(norms, axis=0)

    own_rows = zl * PORTION + c * SUB
    for k in range(2):
        r = slice(k * CH, (k + 1) * CH)
        here = pl.ds(pl.multiple_of(own_rows + k * CH, CH), CH)
        total = part_sum(z, k)
        arrive(rsp.at[3, r], sems("rp", 3, k))
        arrive(rsm.at[3, r], sems("rm", 3, k))
        full = total + rsp[3, r].astype(F32) + rsm[3, r].astype(F32) + dbias[...]
        rec[here] = full.astype(BF16)
        err[z, pl.ds(pl.multiple_of(c * SUB + k * CH, CH), CH)] = (full - acts[here]).astype(BF16)
        mine = rows(err, z, k)
        send(mine, mine, sems("gp", 0, k), at_z(1))
        send(mine, mine, sems("gm", 0, k), at_z(-1))
        send(mine, mine, sems("go", k), partner)

    def relay_err(s):
        for k in range(2):
            for sign, name in ((1, "gp"), (-1, "gm")):
                kept = 0 if sign == 1 else 1
                if s == 3 and k != kept:
                    continue
                part = rows(err, wrap(z - sign * (s + 1), NZ), k)
                arrive(part, sems(name, s, k))
                if s < 2 or (s == 2 and k == kept):
                    send(part, part, sems(name, s + 1, k), at_z(sign))
                send(part, part, sems(name + "c", s, k), partner)

    def err_from_partner(s):
        for k in range(2):
            for sign, name in ((1, "gp"), (-1, "gm")):
                kept = 0 if sign == 1 else 1
                if s == 3 and k != kept:
                    continue
                arrive(rows(err, wrap(z - sign * (s + 1), NZ), k, 1 - c), sems(name + "c", s, k))

    def backward(b, first, last):
        block = err[pl.ds(2 * b, 2)].reshape(ROWS, D)
        weights = wdec[...].reshape(LAT, D)
        back = lax.dot_general(weights, block, NT, preferred_element_type=F32)
        kept = codes_t[b]
        grad_pre = jnp.where(kept.astype(F32) > 0.0, back + SPARSITY * norms, 0.0)
        folded = grad_pre[:, :128] + grad_pre[:, 128:]
        gb[...] = folded if first else gb[...] + folded
        grad_bf = grad_pre.astype(BF16)
        for left, data, acc, pay in ((grad_bf, cent, acc_e, pay_e), (kept, err, acc_d, pay_d)):
            for t in range(0, D, TILE):
                right = data[pl.ds(2 * b, 2), :, t : t + TILE].reshape(ROWS, TILE)
                total = jnp.dot(left, right, preferred_element_type=F32)
                if not first:
                    total = total + acc[:, t : t + TILE]
                if last:
                    pay[:, :, :, t : t + TILE] = total.astype(BF16).reshape(SIDE, SIDE, OWN, TILE)
                else:
                    acc[:, t : t + TILE] = total
            if last and pay is pay_e:
                pay[:, :, :, D : D + 128] = gb[...].astype(BF16).reshape(SIDE, SIDE, OWN, 128)
                pay[:, :, :, D + 128 :] = cs[...].astype(BF16).reshape(SIDE, SIDE, OWN, 128)
            if last:
                (start_e if pay is pay_e else start_d)()

    low, high = pl.ds(0, 2), pl.ds(2, 2)

    def e_part(yy, half):
        return pay_e.at[yy, half]

    def d_part(xx, half):
        return pay_d.at[half, xx]

    def start(part, v, far, close, name, at):
        send(part(wrap(v + 2, SIDE), low), far.at[0], sems(name, "far", 1), at(1))
        send(part(wrap(v + 2, SIDE), high), far.at[1], sems(name, "far", -1), at(-1))
        send(part(wrap(v + 1, SIDE), high), close.at[0, high], sems(name, "own", 1), at(1))
        send(part(wrap(v - 1, SIDE), low), close.at[1, low], sems(name, "own", -1), at(-1))

    def start_e():
        start(e_part, y, e_far, e_near, "e", at_y)

    def start_d():
        start(d_part, x, d_far, d_near, "d", at_x)

    def forward_sum(part, v, far, close, name, at):
        for i, s, half in ((0, 1, low), (1, -1, high)):
            arrive(far.at[i], sems(name, "far", s))
            block = part(wrap(v + s, SIDE), half)
            block[...] = (block[...].astype(F32) + far[i].astype(F32)).astype(BF16)
            send(block, close.at[i, half], sems(name, "sum", s), at(s))

    def at_owner(part, v, w, close, tot, last, name, at):
        for i, s, summed, plain in ((0, 1, low, high), (1, -1, high, low)):
            arrive(close.at[i, plain], sems(name, "own", s))
            arrive(close.at[i, summed], sems(name, "sum", s))
        tot[...] = (
            part(v, pl.ds(0, SIDE))[...].astype(F32) + close[0].astype(F32) + close[1].astype(F32)
        ).astype(BF16)
        for d in (1, 2, 3):
            send(tot.at[wrap(w + d, SIDE)], last.at[d - 1], sems(name, "last", d), at(d))

    def owned(w, tot, last, name):
        total = tot[w].astype(F32)
        for d in (1, 2, 3):
            arrive(last.at[d - 1], sems(name, "last", d))
            total = total + last[d - 1].astype(F32)
        return total

    relay_err(0)
    for k in range(2):
        arrive(rows(err, z, k, 1 - c), sems("go", k))
    err_from_partner(0)
    backward(blocks[0], True, False)
    relay_err(1)
    err_from_partner(1)
    backward(blocks[1], False, False)
    relay_err(2)
    err_from_partner(2)
    backward(blocks[2], False, False)
    relay_err(3)
    own_rec = rec.at[pl.ds(pl.multiple_of(own_rows, SUB), SUB)]
    send(own_rec, own_rec, sems("ro"), partner)
    send(own_rec, own_rec, sems("rz"), pair)
    err_from_partner(3)
    backward(blocks[3], False, True)

    forward_sum(e_part, y, e_far, e_near, "e", at_y)
    forward_sum(d_part, x, d_far, d_near, "d", at_x)
    pair_rec = rec.at[pl.ds(pl.multiple_of((1 - zl) * PORTION + c * SUB, SUB), SUB)]
    arrive(pair_rec, sems("rz"))
    send(pair_rec, pair_rec, sems("rzc"), partner)
    at_owner(e_part, y, x, e_near, tot_e, e_last, "e", at_x)
    at_owner(d_part, x, y, d_near, tot_d, d_last, "d", at_y)
    arrive(rec.at[pl.ds(pl.multiple_of(zl * PORTION + (1 - c) * SUB, SUB), SUB)], sems("ro"))
    arrive(rec.at[pl.ds(pl.multiple_of((1 - zl) * PORTION + (1 - c) * SUB, SUB), SUB)], sems("rzc"))
    recon[...] = rec[...]

    scale = (ROWS * SIDE * SIDE * SIDE) ** -0.5
    total = owned(x, tot_e, e_last, "e")
    genc[...] = scale * total[:, :D]
    bias_sums = scale * jnp.sum(total[:, D : D + 128], axis=1, keepdims=True)
    gbias[...] = jnp.sum(jnp.where(eye, bias_sums, 0.0), axis=0, keepdims=True)
    col_sums = jnp.sum(total[:, D + 128 :], axis=1, keepdims=True)
    mine = dec[...].astype(F32)
    own_norms = jnp.sqrt(jnp.sum(mine * mine, axis=1, keepdims=True) + 1e-06)
    total = owned(y, tot_d, d_last, "d")
    gdec[...] = scale * (total + SPARSITY * col_sums * mine / own_norms)

    for cp in pending:
        cp.wait_send()


def store(*refs):
    sources, results, sem = refs[:4], refs[4:8], refs[8]
    copies = [pltpu.make_async_copy(a, b, sem.at[i]) for i, (a, b) in enumerate(zip(sources, results))]
    for cp in copies:
        cp.start()
    for cp in copies:
        cp.wait()


def per_device(acts, dec_bias, enc_weight, enc_bias, dec_weight):
    vmem, anywhere = pl.BlockSpec(memory_space=pltpu.VMEM), pl.BlockSpec(memory_space=pl.ANY)
    results = (((ROWS, D), BF16), ((OWN, D), F32), ((OWN, D), F32), ((1, OWN), F32))
    in_vmem = pl.pallas_call(
        kernel,
        name="step",
        out_shape=tuple(pltpu.VMEM(*r) for r in results),
        in_specs=[anywhere] * 5,
        out_specs=(vmem,) * 4,
        scratch_shapes=[
            pltpu.VMEM((ROWS, D), F32),
            pltpu.VMEM((1, D), F32),
            pltpu.VMEM((1, OWN), BF16),
            pltpu.VMEM((OWN, D), BF16),
            pltpu.VMEM((NZ, PORTION, D), BF16),
            pltpu.VMEM((SIDE, SIDE, OWN, WE), BF16),
            pltpu.VMEM((SIDE, SIDE, OWN, D), BF16),
            pltpu.VMEM((SIDE, 2, PORTION, LAT), BF16),
            pltpu.VMEM((SIDE, LAT, ROWS), BF16),
            pltpu.VMEM((NZ, SUB, D), F32),
            pltpu.VMEM((NZ, SUB, D), BF16),
            pltpu.VMEM((NZ, SUB, D), BF16),
            pltpu.VMEM((NZ, SUB, D), BF16),
            pltpu.VMEM((4, SUB, D), BF16),
            pltpu.VMEM((4, SUB, D), BF16),
            pltpu.VMEM((NZ, PORTION, D), BF16),
            pltpu.VMEM((LAT, D), F32),
            pltpu.VMEM((LAT, D), F32),
            pltpu.VMEM((LAT, 128), F32),
            pltpu.VMEM((LAT, 128), F32),
            pltpu.VMEM((SIDE, SIDE, OWN, GE), BF16),
            pltpu.VMEM((SIDE, SIDE, OWN, D), BF16),
            pltpu.VMEM((2, 2, OWN, GE), BF16),
            pltpu.VMEM((2, SIDE, OWN, GE), BF16),
            pltpu.VMEM((SIDE, OWN, GE), BF16),
            pltpu.VMEM((3, OWN, GE), BF16),
            pltpu.VMEM((2, 2, OWN, D), BF16),
            pltpu.VMEM((2, SIDE, OWN, D), BF16),
            pltpu.VMEM((SIDE, OWN, D), BF16),
            pltpu.VMEM((3, OWN, D), BF16),
            pltpu.VMEM((ROWS, D), BF16),
            pltpu.SemaphoreType.DMA((5,)),
            pltpu.SemaphoreType.DMA((N_SEMS,)),
            pltpu.SemaphoreType.DMA((N_SEMS,)),
        ],
        compiler_params=pltpu.CompilerParams(collective_id=0, has_side_effects=True, vmem_limit_bytes=60 << 20),
    )(acts, dec_bias[None, :], enc_weight, enc_bias[None, :], dec_weight)
    recon, genc, gdec, gbias = pl.pallas_call(
        store,
        name="store",
        out_shape=tuple(jax.ShapeDtypeStruct(*r) for r in results),
        in_specs=[vmem] * 4,
        out_specs=(anywhere,) * 4,
        scratch_shapes=[pltpu.SemaphoreType.DMA((4,))],
    )(*[pltpu.with_memory_space_constraint(r, pltpu.VMEM) for r in in_vmem])
    return recon, genc, gdec, gbias[0]


def solution(mesh):
    torus = Mesh(mesh.devices.reshape(2, 2, SIDE, SIDE, SIDE), AXES)
    wide = P(("y", "x", "h"), None)
    return jax.shard_map(
        per_device,
        mesh=torus,
        in_specs=(wide, P(), P(AXES, None), P(AXES), P(AXES, None)),
        out_specs=(wide, P(AXES, None), P(AXES, None), P(AXES)),
        check_vma=False,
    )
```

```python
import jax
import jax.numpy as jnp
from jax import lax
from jax.experimental import pallas as pl
from jax.experimental.pallas import tpu as pltpu
from jax.sharding import Mesh
from jax.sharding import PartitionSpec as P


AXES = ("zl", "c", "y", "x", "h")
MESH = pl.DeviceIdType.MESH
F32, BF16 = jnp.float32, jnp.bfloat16
SPARSITY = 0.5
NZ, SIDE, ROWS, D, OWN, LAT = 8, 4, 256, 2048, 16, 256
PORTION = ROWS // 2
SUB = PORTION // 2
CH = SUB // 2
STRIP = CH // 2
WE = D + 128
STATS = 256
GE = STATS + D
TILE = 512


class Semaphores:
    def __init__(self):
        self.names = {}

    def __call__(self, *name):
        return self.names.setdefault(name, len(self.names))


N_ARRIVE, N_LEAVE = 104, 18
NT = (((1,), (1,)), ((), ()))


def kernel(
    acts_hbm, dbias_hbm, enc_hbm, bias_hbm, dec_hbm, recon, genc, gdec, gbias, acts, dbias, bias, dec,
    cent, wenc, wdec, codes, codes_t, pown, psend, precv, psum, rsp, rsm, err, acc_e, acc_d, gb, cs,
    pay_e, pay_d, e_far, e_near, tot_e, e_last, d_far, d_near, tot_d, d_last, rec, lsem, ssem, rsem,
):
    zl, c, y, x, h = [lax.axis_index(a) for a in AXES]
    z = 2 * h + zl
    sems, kinds = Semaphores(), Semaphores()

    def wrap(v, n):
        return lax.rem(v + 2 * n, n)

    def at_z(dz):
        q = wrap(z + dz, NZ)
        return (lax.rem(q, 2), c, y, x, lax.div(q, 2))

    def at_y(dy):
        return (zl, c, wrap(y + dy, SIDE), x, h)

    def at_x(dx):
        return (zl, c, y, wrap(x + dx, SIDE), h)

    partner = (zl, 1 - c, y, x, h)
    pair = (1 - zl, c, y, x, h)

    def copy(src, dst, dev, leaves, arrives):
        return pltpu.make_async_remote_copy(
            src_ref=src, dst_ref=dst, send_sem=ssem.at[leaves], recv_sem=rsem.at[arrives], device_id=dev, device_id_type=MESH
        )

    def send(src, dst, arrives, dev, kind):
        copy(src, dst, dev, kinds(kind), arrives).start()

    def arrive(dst, sem):
        copy(dst, dst, partner, 0, sem).wait_recv()

    def left(src, kind):
        copy(src, src, partner, kinds(kind), 0).wait_send()

    def rows(ref, p, k, core=None):
        return ref.at[k, p, c if core is None else core]

    loads = [
        pltpu.make_async_copy(src, dst, lsem.at[i])
        for i, (src, dst) in enumerate(
            (
                (bias_hbm, bias),
                (enc_hbm, wenc.at[y, x, :, pl.ds(0, D)]),
                (dec_hbm, dec),
                (dbias_hbm, dbias),
                (acts_hbm, acts),
            )
        )
    ]
    for load in loads:
        load.start()
    barrier = pltpu.get_barrier_semaphore()
    friends = [partner, at_z(1), at_z(-1)] + [at_y(d) for d in (1, 2, 3)] + [at_x(d) for d in (1, 2, 3)]
    for f in friends:
        pl.semaphore_signal(barrier, inc=1, device_id=f, device_id_type=MESH)
    for load in loads:
        load.wait()
    for q in range(2):
        for who in range(2):
            for k in range(2):
                at = q * PORTION + who * SUB + k * CH
                cent[k, 2 * h + q, who] = (acts[at : at + CH] - dbias[...]).astype(BF16)
    eye = lax.broadcasted_iota(jnp.int32, (OWN, OWN), 0) == lax.broadcasted_iota(jnp.int32, (OWN, OWN), 1)
    column = jnp.sum(jnp.where(eye, bias[...].astype(F32), 0.0), axis=1, keepdims=True)
    wenc[y, x, :, D:] = jnp.broadcast_to(column, (OWN, 128)).astype(BF16)
    wdec[y, x] = dec[...]
    pl.semaphore_wait(barrier, len(friends))

    for d in (1, 2, 3):
        send(wenc.at[y, x], wenc.at[y, x], sems("we1"), at_x(d), "we1")
        send(dec, wdec.at[y, x], sems("wd1"), at_y(d), "wd1")

    def mirrored(even, odd):
        return wrap(2 * h + even + zl * (odd - even), NZ)

    coming = {
        "a": [mirrored(-2, 3), mirrored(-1, 2), mirrored(-4, 5)],
        "b": [mirrored(3, -2), mirrored(2, -1), mirrored(5, -4)],
    }
    outer = at_z(2 * zl - 1)

    def piece(p, k):
        return rows(cent, p, k)

    def send_own(j, k):
        part = piece(mirrored(1 - j, j), k)
        send(part, part, sems("a", j, k), outer, "acts")

    send_own(0, 0)
    send_own(1, 0)
    send_own(0, 1)

    def relay_acts(name, j, k):
        part = piece(coming[name][j], k)
        arrive(part, sems(name, j, k))
        if name == "a":
            send(part, part, sems("b", j, k), pair, "acts")
        elif j == 0:
            send(part, part, sems("a", 2, k), outer, "acts")
        send(part, part, sems("early" if name == "a" and j < 2 else "late", k), partner, "acts")

    def from_partner(which, k):
        arrive(cent.at[0, pl.ds(0, 1 if which == "early" else 2)], sems(which, k))

    relay_acts("a", 0, 0)
    arrive(wenc.at[0, pl.ds(0, 3)], sems("we1"))
    arrive(wdec.at[0, pl.ds(0, 3)], sems("wd1"))
    for i in range(2):
        for s in (1, -1):
            half = pl.ds(0 if (s == 1) == (i == 0) else 2, 2)
            order = s if i == 0 else 0
            send(wenc.at[y, half], wenc.at[y, half], sems("we2", order), at_y(s), "we2")
            send(wdec.at[half, x], wdec.at[half, x], sems("wd2", order), at_x(s), "wd2")
    relay_acts("a", 1, 0)
    relay_acts("b", 0, 0)
    send_own(1, 1)
    relay_acts("a", 0, 1)
    relay_acts("b", 1, 0)
    for s in (1, -1):
        half = pl.ds(0 if s == 1 else 2, 2)
        yn, xn = wrap(y - s, SIDE), wrap(x - s, SIDE)
        arrive(wenc.at[yn, half], sems("we2", s))
        send(wenc.at[yn, half], wenc.at[yn, half], sems("we2", 0), at_y(s), "we2")
        arrive(wdec.at[half, xn], sems("wd2", s))
        send(wdec.at[half, xn], wdec.at[half, xn], sems("wd2", 0), at_x(s), "wd2")
    relay_acts("a", 2, 0)
    relay_acts("b", 0, 1)
    relay_acts("a", 1, 1)
    arrive(wenc.at[pl.ds(0, 2)], sems("we2", 0))
    arrive(wdec.at[pl.ds(0, 2)], sems("wd2", 0))

    def encode(k, pair_of):
        block = jnp.concatenate([cent[k, pl.ds(2 * b, 2)].reshape(PORTION, D) for b in pair_of], axis=0)
        weights = wenc[:, :, :, :D].reshape(LAT, D)
        shift = wenc[:, :, :, D:].reshape(LAT, 128).astype(F32)
        pre = lax.dot_general(weights, block, NT, preferred_element_type=F32)
        value = jnp.maximum(pre + jnp.concatenate([shift, shift], axis=1), 0.0)
        turned = value.T.astype(BF16)
        for i, b in enumerate(pair_of):
            for q in range(2):
                for who in range(2):
                    at = i * PORTION + q * SUB + who * CH
                    codes[k, b, who, q * CH : (q + 1) * CH] = turned[at : at + CH]
            codes_t[k, b] = value[:, i * PORTION : (i + 1) * PORTION].astype(BF16)
        folded = value[:, :128] + value[:, 128:]
        cs[...] = folded if k == 0 and pair_of is early else cs[...] + folded

    def decode(k, pair_of):
        left = [jnp.concatenate([codes[k, b, who] for b in pair_of], axis=0) for who in (1 - c, c)]
        for t in range(0, D, TILE):
            right = wdec[:, :, :, t : t + TILE].reshape(LAT, TILE)
            other = jnp.dot(left[0], right, preferred_element_type=F32).astype(BF16)
            mine = jnp.dot(left[1], right, preferred_element_type=F32)
            for i, b in enumerate(pair_of):
                for q in range(2):
                    r = slice((2 * i + q) * CH, (2 * i + q + 1) * CH)
                    psend[k, 2 * b + q, :, t : t + TILE] = other[r]
                    pown[k, 2 * b + q, :, t : t + TILE] = mine[r]
        for i, b in enumerate(pair_of):
            for q in range(2):
                part = precv.at[k, 2 * b + q]
                send(psend.at[k, 2 * b + q], part, sems("px", k), partner, "px")

    def decoded(k):
        arrive(precv.at[k], sems("px", k))

    def strip(r):
        return pl.ds(r * STRIP, STRIP)

    def farthest(sign, r):
        return (sign == 1) == (r == 0)

    def part_sum(k, p, r):
        return pown[k, p, strip(r)] + precv[k, p, strip(r)].astype(F32)

    def pass_on(sign, k, r, away):
        buf, name = (rsp, "rp") if sign == 1 else (rsm, "rm")
        p = wrap(z + sign * away, NZ)
        part = psum.at[k, p, strip(r)]
        total = part_sum(k, p, r)
        if away < (4 if farthest(sign, r) else 3):
            arrive(buf.at[k, away, strip(r)], sems(name, k, r, away + 1))
            total = total + buf[k, away, strip(r)].astype(F32)
        part[...] = total.astype(BF16)
        send(part, buf.at[k, away - 1, strip(r)], sems(name, k, r, away), at_z(sign), "sums")

    def steps(k, *which):
        for n in which:
            r, away = ((0, 4), (1, 3), (0, 3), (1, 2), (0, 2), (1, 1), (0, 1))[n - 1]
            pass_on(1, k, r, away)
            pass_on(-1, k, 1 - r, away)

    near = 1 - 2 * zl
    blocks = [h, wrap(h - near, SIDE), wrap(h + near, SIDE), wrap(h + 2, SIDE)]
    early, late = tuple(blocks[:2]), tuple(blocks[2:])
    relay_acts("b", 2, 0)
    from_partner("early", 0)
    encode(0, early)
    relay_acts("a", 2, 1)
    decode(0, early)
    from_partner("late", 0)
    encode(0, late)
    decode(0, late)
    relay_acts("b", 1, 1)
    from_partner("early", 1)
    encode(1, early)
    decoded(0)
    steps(0, 1, 2)
    decode(1, early)
    relay_acts("b", 2, 1)
    from_partner("late", 1)
    encode(1, late)
    decode(1, late)
    steps(0, 3, 4)
    decoded(1)
    for n, m in ((1, 5), (2, 6)):
        steps(1, n)
        steps(0, m)
    steps(0, 7)
    steps(1, 3, 4)

    own_rows = zl * PORTION + c * SUB

    def at_home(k):
        for r in range(2):
            at = k * CH + r * STRIP
            here = pl.ds(pl.multiple_of(own_rows + at, STRIP), STRIP)
            total = part_sum(k, z, r) + dbias[...]
            arrive(rsp.at[k, 0, strip(r)], sems("rp", k, r, 1))
            arrive(rsm.at[k, 0, strip(r)], sems("rm", k, r, 1))
            full = total + rsp[k, 0, strip(r)].astype(F32) + rsm[k, 0, strip(r)].astype(F32)
            rec[here] = full.astype(BF16)
            err[k, z, c, strip(r)] = (full - acts[here]).astype(BF16)
            mine = rows(err, z, k).at[strip(r)]
            send(mine, mine, sems("gp", 0, k, r), at_z(1), "err")
            send(mine, mine, sems("gm", 0, k, r), at_z(-1), "err")
            send(mine, mine, sems("errc", 0), partner, "errc")

    at_home(0)
    steps(1, 5, 6, 7)

    norms = []
    for q in range(2):
        rows_q = wdec[2 * q : 2 * q + 2].reshape(LAT // 2, D).astype(F32)
        norms.append(jnp.sqrt(jnp.sum(rows_q * rows_q, axis=1, keepdims=True) + 1e-06))
    norms = jnp.concatenate(norms, axis=0)

    def incoming(s, k, r, sign, core=None):
        return rows(err, wrap(z - sign * (s + 1), NZ), k, core).at[strip(r)]

    def relay_err(s, k):
        for r in range(2):
            for sign, name in ((1, "gp"), (-1, "gm")):
                if s == 3 and not farthest(sign, r):
                    continue
                part = incoming(s, k, r, sign)
                arrive(part, sems(name, s, k, r))
                if s < 2 or (s == 2 and farthest(sign, r)):
                    send(part, part, sems(name, s + 1, k, r), at_z(sign), "err")
                send(part, part, sems("errc", s), partner, "errc")

    def err_from_partner(s):
        arrive(err.at[0, pl.ds(0, (3, 2, 2, 1)[s])], sems("errc", s))

    def backward(b, first, last):
        block = err[:, pl.ds(2 * b, 2)].reshape(ROWS, D)
        weights = wdec[...].reshape(LAT, D)
        back = lax.dot_general(weights, block, NT, preferred_element_type=F32)
        kept = jnp.concatenate([codes_t[0, b], codes_t[1, b]], axis=1)
        grad_pre = jnp.where(kept.astype(F32) > 0.0, back + SPARSITY * norms, 0.0)
        folded = grad_pre[:, :128] + grad_pre[:, 128:]
        gb[...] = folded if first else gb[...] + folded
        grad_bf = grad_pre.astype(BF16)
        if last:
            pay_e[:, :, :, :128] = gb[...].astype(BF16).reshape(SIDE, SIDE, OWN, 128)
            pay_e[:, :, :, 128:STATS] = cs[...].astype(BF16).reshape(SIDE, SIDE, OWN, 128)
        for left, data, acc, pay in ((grad_bf, cent, acc_e, pay_e), (kept, err, acc_d, pay_d)):
            for t in range(0, D, TILE):
                right = data[:, pl.ds(2 * b, 2), :, :, t : t + TILE].reshape(ROWS, TILE)
                total = jnp.dot(left, right, preferred_element_type=F32)
                if not first:
                    total = total + acc[:, t : t + TILE]
                if not last:
                    acc[:, t : t + TILE] = total
                    continue
                at = t + (STATS if pay is pay_e else 0)
                pay[:, :, :, at : at + TILE] = total.astype(BF16).reshape(SIDE, SIDE, OWN, TILE)
                if t % (D // 2) == D // 2 - TILE:
                    (start_e if pay is pay_e else start_d)(2 * t // D)

    low, high = pl.ds(0, 2), pl.ds(2, 2)

    def e_part(yy, half, cols):
        return pay_e.at[yy, half, :, cols]

    def d_part(xx, half, cols):
        return pay_d.at[half, xx, :, cols]

    E_COLS = [pl.ds(0, STATS + D // 2), pl.ds(STATS + D // 2, D // 2)]
    D_COLS = [pl.ds(0, D // 2), pl.ds(D // 2, D // 2)]

    def start(i, cols, part, v, far, close, name, at):
        for n, s, summed, plain in ((0, 1, low, high), (1, -1, high, low)):
            send(part(wrap(v + 2, SIDE), summed, cols), far.at[n, :, :, cols], sems(name, "far", s, i), at(s), (name, i))
        for n, s, summed, plain in ((0, 1, low, high), (1, -1, high, low)):
            send(part(wrap(v + s, SIDE), plain, cols), close.at[n, plain, :, cols], sems(name, "near", i), at(s), (name, i))

    def start_e(i):
        start(i, E_COLS[i], e_part, y, e_far, e_near, "e", at_y)

    def start_d(i):
        start(i, D_COLS[i], d_part, x, d_far, d_near, "d", at_x)

    def forward_sum(i, cols, part, v, far, close, name, at):
        for n, s, half in ((0, 1, low), (1, -1, high)):
            arrive(far.at[n, :, :, cols], sems(name, "far", s, i))
            block = part(wrap(v + s, SIDE), half, cols)
            block[...] = (block[...].astype(F32) + far[n, :, :, cols].astype(F32)).astype(BF16)
            send(block, close.at[n, half, :, cols], sems(name, "near", i), at(s), (name, i))

    def at_owner(i, cols, part, v, w, close, tot, last, name, at):
        arrive(close.at[:, :, :, cols], sems(name, "near", i))
        tot[:, :, cols] = (
            part(v, pl.ds(0, SIDE), cols)[...].astype(F32)
            + close[0, :, :, cols].astype(F32)
            + close[1, :, :, cols].astype(F32)
        ).astype(BF16)
        for d in (2, 1, 3):
            send(tot.at[wrap(w + d, SIDE), :, cols], last.at[d - 1, :, cols], sems(name, "last", i), at(d), (name, "last", i))

    def owned(i, cols, w, tot, last, name):
        total = tot[w, :, cols].astype(F32)
        arrive(last.at[:, :, cols], sems(name, "last", i))
        for d in (1, 2, 3):
            total = total + last[d - 1, :, cols].astype(F32)
        return total

    relay_err(0, 0)
    at_home(1)
    relay_err(1, 0)
    relay_err(0, 1)
    relay_err(2, 0)
    relay_err(1, 1)
    err_from_partner(0)
    backward(blocks[0], True, False)
    relay_err(3, 0)
    err_from_partner(1)
    backward(blocks[1], False, False)
    relay_err(2, 1)
    err_from_partner(2)
    backward(blocks[2], False, False)
    relay_err(3, 1)
    own_rec = rec.at[pl.ds(pl.multiple_of(own_rows, SUB), SUB)]
    send(own_rec, own_rec, sems("rc"), partner, "rec")
    send(own_rec, own_rec, sems("rz"), pair, "rec")
    err_from_partner(3)
    backward(blocks[3], False, True)

    for i in range(2):
        forward_sum(i, E_COLS[i], e_part, y, e_far, e_near, "e", at_y)
        forward_sum(i, D_COLS[i], d_part, x, d_far, d_near, "d", at_x)
    pair_rec = rec.at[pl.ds(pl.multiple_of((1 - zl) * PORTION + c * SUB, SUB), SUB)]
    arrive(pair_rec, sems("rz"))
    send(pair_rec, pair_rec, sems("rc"), partner, "rec")
    for i in range(2):
        at_owner(i, E_COLS[i], e_part, y, x, e_near, tot_e, e_last, "e", at_x)
        at_owner(i, D_COLS[i], d_part, x, y, d_near, tot_d, d_last, "d", at_y)
    arrive(rec.at[pl.ds(0, 2 * SUB)], sems("rc"))
    recon[...] = rec[...]

    scale = (ROWS * SIDE * SIDE * SIDE) ** -0.5
    mine = dec[...].astype(F32)
    own_norms = jnp.sqrt(jnp.sum(mine * mine, axis=1, keepdims=True) + 1e-06)
    sides = [pl.ds(0, D // 2), pl.ds(D // 2, D // 2)]
    for i in range(2):
        total = owned(i, E_COLS[i], x, tot_e, e_last, "e")
        genc[:, sides[i]] = scale * (total[:, STATS:] if i == 0 else total)
        if i == 0:
            bias_sums = scale * jnp.sum(total[:, :128], axis=1, keepdims=True)
            gbias[...] = jnp.sum(jnp.where(eye, bias_sums, 0.0), axis=0, keepdims=True)
            sparse = SPARSITY * jnp.sum(total[:, 128:STATS], axis=1, keepdims=True) * mine / own_norms
        total = owned(i, D_COLS[i], y, tot_d, d_last, "d")
        gdec[:, sides[i]] = scale * (total + sparse[:, i * (D // 2) : (i + 1) * (D // 2)])

    left(wenc.at[0, pl.ds(0, 3)], "we1")
    left(wdec.at[0, pl.ds(0, 3)], "wd1")
    left(wenc.at[pl.ds(0, 3)], "we2")
    left(wdec.at[pl.ds(0, 3)], "wd2")
    left(cent.at[:, pl.ds(0, 6)], "acts")
    left(cent.at[0], "px")
    left(cent.at[0, pl.ds(0, 7)], "sums")
    left(cent.at[0, pl.ds(0, 7)], "err")
    left(cent.at[0], "errc")
    left(rec.at[pl.ds(0, 3 * SUB)], "rec")
    for i in range(2):
        left(pay_e.at[pl.ds(0, 3), :, :, E_COLS[i]], ("e", i))
        left(pay_d.at[pl.ds(0, 3), :, :, D_COLS[i]], ("d", i))
        left(tot_e.at[pl.ds(0, 3), :, E_COLS[i]], ("e", "last", i))
        left(tot_d.at[pl.ds(0, 3), :, D_COLS[i]], ("d", "last", i))
    assert (len(sems.names), len(kinds.names)) == (N_ARRIVE, N_LEAVE)


def store(*refs):
    sources, results, sem = refs[:4], refs[4:8], refs[8]
    copies = [pltpu.make_async_copy(a, b, sem.at[i]) for i, (a, b) in enumerate(zip(sources, results))]
    for cp in copies:
        cp.start()
    for cp in copies:
        cp.wait()


def per_device(acts, dec_bias, enc_weight, enc_bias, dec_weight):
    vmem, anywhere = pl.BlockSpec(memory_space=pltpu.VMEM), pl.BlockSpec(memory_space=pl.ANY)
    results = (((ROWS, D), BF16), ((OWN, D), F32), ((OWN, D), F32), ((1, OWN), F32))
    in_vmem = pl.pallas_call(
        kernel,
        name="step",
        out_shape=tuple(pltpu.VMEM(*r) for r in results),
        in_specs=[anywhere] * 5,
        out_specs=(vmem,) * 4,
        scratch_shapes=[
            pltpu.VMEM((ROWS, D), F32),
            pltpu.VMEM((1, D), F32),
            pltpu.VMEM((1, OWN), BF16),
            pltpu.VMEM((OWN, D), BF16),
            pltpu.VMEM((2, NZ, 2, CH, D), BF16),
            pltpu.VMEM((SIDE, SIDE, OWN, WE), BF16),
            pltpu.VMEM((SIDE, SIDE, OWN, D), BF16),
            pltpu.VMEM((2, SIDE, 2, SUB, LAT), BF16),
            pltpu.VMEM((2, SIDE, LAT, PORTION), BF16),
            pltpu.VMEM((2, NZ, CH, D), F32),
            pltpu.VMEM((2, NZ, CH, D), BF16),
            pltpu.VMEM((2, NZ, CH, D), BF16),
            pltpu.VMEM((2, NZ, CH, D), BF16),
            pltpu.VMEM((2, 4, CH, D), BF16),
            pltpu.VMEM((2, 4, CH, D), BF16),
            pltpu.VMEM((2, NZ, 2, CH, D), BF16),
            pltpu.VMEM((LAT, D), F32),
            pltpu.VMEM((LAT, D), F32),
            pltpu.VMEM((LAT, 128), F32),
            pltpu.VMEM((LAT, 128), F32),
            pltpu.VMEM((SIDE, SIDE, OWN, GE), BF16),
            pltpu.VMEM((SIDE, SIDE, OWN, D), BF16),
            pltpu.VMEM((2, 2, OWN, GE), BF16),
            pltpu.VMEM((2, SIDE, OWN, GE), BF16),
            pltpu.VMEM((SIDE, OWN, GE), BF16),
            pltpu.VMEM((3, OWN, GE), BF16),
            pltpu.VMEM((2, 2, OWN, D), BF16),
            pltpu.VMEM((2, SIDE, OWN, D), BF16),
            pltpu.VMEM((SIDE, OWN, D), BF16),
            pltpu.VMEM((3, OWN, D), BF16),
            pltpu.VMEM((ROWS, D), BF16),
            pltpu.SemaphoreType.DMA((5,)),
            pltpu.SemaphoreType.DMA((N_LEAVE,)),
            pltpu.SemaphoreType.DMA((N_ARRIVE,)),
        ],
        compiler_params=pltpu.CompilerParams(collective_id=0, has_side_effects=True, vmem_limit_bytes=60 << 20),
    )(acts, dec_bias[None, :], enc_weight, enc_bias[None, :], dec_weight)
    recon, genc, gdec, gbias = pl.pallas_call(
        store,
        name="store",
        out_shape=tuple(jax.ShapeDtypeStruct(*r) for r in results),
        in_specs=[vmem] * 4,
        out_specs=(anywhere,) * 4,
        scratch_shapes=[pltpu.SemaphoreType.DMA((4,))],
    )(*[pltpu.with_memory_space_constraint(r, pltpu.VMEM) for r in in_vmem])
    return recon, genc, gdec, gbias[0]


def solution(mesh):
    torus = Mesh(mesh.devices.reshape(2, 2, SIDE, SIDE, SIDE), AXES)
    wide = P(("y", "x", "h"), None)
    return jax.shard_map(
        per_device,
        mesh=torus,
        in_specs=(wide, P(), P(AXES, None), P(AXES), P(AXES, None)),
        out_specs=(wide, P(AXES, None), P(AXES, None), P(AXES)),
        check_vma=False,
    )
```

```python
import jax
import jax.numpy as jnp
from jax import lax
from jax.experimental import pallas as pl
from jax.experimental.pallas import tpu as pltpu
from jax.sharding import Mesh
from jax.sharding import PartitionSpec as P


AXES = ("zl", "c", "y", "x", "h")
MESH = pl.DeviceIdType.MESH
F32, BF16 = jnp.float32, jnp.bfloat16
SPARSITY = 0.5
NZ, SIDE, ROWS, D, OWN, LAT = 8, 4, 256, 2048, 16, 256
PORTION = ROWS // 2
SUB = PORTION // 2
CH = SUB // 2
STRIP = CH // 2
WE = D + 128
STATS = 256
GE = STATS + D
TILE = 512


class Semaphores:
    def __init__(self):
        self.names = {}

    def __call__(self, *name):
        return self.names.setdefault(name, len(self.names))


N_ARRIVE, N_LEAVE = 105, 18
NT = (((1,), (1,)), ((), ()))


def kernel(
    acts_hbm, dbias_hbm, enc_hbm, bias_hbm, dec_hbm, recon, genc, gdec, gbias, acts, dbias, bias, dec,
    cent, wenc, wdec, codes, codes_t, pown, psend, precv, psum, rsp, rsm, err, acc_e, acc_d, gb, cs,
    pay_e, pay_d, e_far, e_near, tot_e, e_last, d_far, d_near, tot_d, d_last, rec, lsem, ssem, rsem,
):
    zl, c, y, x, h = [lax.axis_index(a) for a in AXES]
    z = 2 * h + zl
    sems, kinds = Semaphores(), Semaphores()

    def wrap(v, n):
        return lax.rem(v + 2 * n, n)

    def at_z(dz):
        q = wrap(z + dz, NZ)
        return (lax.rem(q, 2), c, y, x, lax.div(q, 2))

    def at_y(dy):
        return (zl, c, wrap(y + dy, SIDE), x, h)

    def at_x(dx):
        return (zl, c, y, wrap(x + dx, SIDE), h)

    partner = (zl, 1 - c, y, x, h)
    pair = (1 - zl, c, y, x, h)

    def copy(src, dst, dev, leaves, arrives):
        return pltpu.make_async_remote_copy(
            src_ref=src, dst_ref=dst, send_sem=ssem.at[leaves], recv_sem=rsem.at[arrives], device_id=dev, device_id_type=MESH
        )

    def send(src, dst, arrives, dev, kind):
        copy(src, dst, dev, kinds(kind), arrives).start()

    def arrive(dst, sem):
        copy(dst, dst, partner, 0, sem).wait_recv()

    def left(src, kind):
        copy(src, src, partner, kinds(kind), 0).wait_send()

    def rows(ref, p, k, core=None):
        return ref.at[k, p, c if core is None else core]

    loads = [
        pltpu.make_async_copy(src, dst, lsem.at[i])
        for i, (src, dst) in enumerate(
            (
                (bias_hbm, bias),
                (enc_hbm, wenc.at[y, x, :, pl.ds(0, D)]),
                (dec_hbm, dec),
                (dbias_hbm, dbias),
                (acts_hbm, acts),
            )
        )
    ]
    for load in loads:
        load.start()
    barrier = pltpu.get_barrier_semaphore()
    friends = [partner, at_z(1), at_z(-1)] + [at_y(d) for d in (1, 2, 3)] + [at_x(d) for d in (1, 2, 3)]
    for f in friends:
        pl.semaphore_signal(barrier, inc=1, device_id=f, device_id_type=MESH)
    for load in loads:
        load.wait()
    for q in range(2):
        for who in range(2):
            for k in range(2):
                at = q * PORTION + who * SUB + k * CH
                cent[k, 2 * h + q, who] = (acts[at : at + CH] - dbias[...]).astype(BF16)
    eye = lax.broadcasted_iota(jnp.int32, (OWN, OWN), 0) == lax.broadcasted_iota(jnp.int32, (OWN, OWN), 1)
    column = jnp.sum(jnp.where(eye, bias[...].astype(F32), 0.0), axis=1, keepdims=True)
    wenc[y, x, :, D:] = jnp.broadcast_to(column, (OWN, 128)).astype(BF16)
    wdec[y, x] = dec[...]
    pl.semaphore_wait(barrier, len(friends))

    for d in (1, 2, 3):
        send(wenc.at[y, x], wenc.at[y, x], sems("we1"), at_x(d), "we1")
        send(dec, wdec.at[y, x], sems("wd1"), at_y(d), "wd1")

    def mirrored(even, odd):
        return wrap(2 * h + even + zl * (odd - even), NZ)

    coming = {
        "a": [mirrored(-2, 3), mirrored(-1, 2), mirrored(-4, 5)],
        "b": [mirrored(3, -2), mirrored(2, -1), mirrored(5, -4)],
    }
    outer = at_z(2 * zl - 1)

    def piece(p, k):
        return rows(cent, p, k)

    def send_own(j, k):
        part = piece(mirrored(1 - j, j), k)
        send(part, part, sems("a", j, k), outer, "acts")

    send_own(0, 0)
    send_own(1, 0)
    send_own(0, 1)

    def relay_acts(name, j, k):
        part = piece(coming[name][j], k)
        arrive(part, sems(name, j, k))
        if name == "a":
            send(part, part, sems("b", j, k), pair, "acts")
        elif j == 0:
            send(part, part, sems("a", 2, k), outer, "acts")
        send(part, part, sems("early" if name == "a" and j < 2 else "late", k), partner, "acts")

    def from_partner(which, k):
        arrive(cent.at[0, pl.ds(0, 1 if which == "early" else 2)], sems(which, k))

    relay_acts("a", 0, 0)
    arrive(wenc.at[0, pl.ds(0, 3)], sems("we1"))
    arrive(wdec.at[0, pl.ds(0, 3)], sems("wd1"))
    for i in range(2):
        for s in (1, -1):
            half = pl.ds(0 if (s == 1) == (i == 0) else 2, 2)
            order = s if i == 0 else 0
            send(wenc.at[y, half], wenc.at[y, half], sems("we2", order), at_y(s), "we2")
            send(wdec.at[half, x], wdec.at[half, x], sems("wd2", order), at_x(s), "wd2")
    relay_acts("a", 1, 0)
    relay_acts("b", 0, 0)
    send_own(1, 1)
    relay_acts("a", 0, 1)
    relay_acts("b", 1, 0)
    for s in (1, -1):
        half = pl.ds(0 if s == 1 else 2, 2)
        yn, xn = wrap(y - s, SIDE), wrap(x - s, SIDE)
        arrive(wenc.at[yn, half], sems("we2", s))
        send(wenc.at[yn, half], wenc.at[yn, half], sems("we2", 0), at_y(s), "we2")
        arrive(wdec.at[half, xn], sems("wd2", s))
        send(wdec.at[half, xn], wdec.at[half, xn], sems("wd2", 0), at_x(s), "wd2")
    relay_acts("a", 2, 0)
    relay_acts("b", 0, 1)
    relay_acts("a", 1, 1)
    arrive(wenc.at[pl.ds(0, 2)], sems("we2", 0))
    arrive(wdec.at[pl.ds(0, 2)], sems("wd2", 0))

    def encode(k, pair_of):
        block = jnp.concatenate([cent[k, pl.ds(2 * b, 2)].reshape(PORTION, D) for b in pair_of], axis=0)
        weights = wenc[:, :, :, :D].reshape(LAT, D)
        shift = wenc[:, :, :, D:].reshape(LAT, 128).astype(F32)
        pre = lax.dot_general(weights, block, NT, preferred_element_type=F32)
        value = jnp.maximum(pre + jnp.concatenate([shift, shift], axis=1), 0.0)
        turned = value.T.astype(BF16)
        for i, b in enumerate(pair_of):
            for q in range(2):
                for who in range(2):
                    at = i * PORTION + q * SUB + who * CH
                    codes[k, b, who, q * CH : (q + 1) * CH] = turned[at : at + CH]
            codes_t[k, b] = value[:, i * PORTION : (i + 1) * PORTION].astype(BF16)
        folded = value[:, :128] + value[:, 128:]
        cs[...] = folded if k == 0 and pair_of is early else cs[...] + folded

    def decode(k, pair_of):
        left = [jnp.concatenate([codes[k, b, who] for b in pair_of], axis=0) for who in (1 - c, c)]
        for t in range(0, D, TILE):
            right = wdec[:, :, :, t : t + TILE].reshape(LAT, TILE)
            other = jnp.dot(left[0], right, preferred_element_type=F32).astype(BF16)
            mine = jnp.dot(left[1], right, preferred_element_type=F32)
            for i, b in enumerate(pair_of):
                for q in range(2):
                    r = slice((2 * i + q) * CH, (2 * i + q + 1) * CH)
                    psend[k, 2 * b + q, :, t : t + TILE] = other[r]
                    pown[k, 2 * b + q, :, t : t + TILE] = mine[r]
        for i, b in enumerate(pair_of):
            for q in range(2):
                part = precv.at[k, 2 * b + q]
                send(psend.at[k, 2 * b + q], part, sems("px", k), partner, "px")

    def decoded(k):
        arrive(precv.at[k], sems("px", k))

    def strip(r):
        return pl.ds(r * STRIP, STRIP)

    def farthest(sign, r):
        return (sign == 1) == (r == 0)

    def part_sum(k, p, r):
        return pown[k, p, strip(r)] + precv[k, p, strip(r)].astype(F32)

    def pass_on(sign, k, r, away):
        buf, name = (rsp, "rp") if sign == 1 else (rsm, "rm")
        p = wrap(z + sign * away, NZ)
        part = psum.at[k, p, strip(r)]
        total = part_sum(k, p, r)
        if away < (4 if farthest(sign, r) else 3):
            arrive(buf.at[k, away, strip(r)], sems(name, k, r, away + 1))
            total = total + buf[k, away, strip(r)].astype(F32)
        part[...] = total.astype(BF16)
        send(part, buf.at[k, away - 1, strip(r)], sems(name, k, r, away), at_z(sign), "sums")

    def steps(k, *which):
        for n in which:
            r, away = ((0, 4), (1, 3), (0, 3), (1, 2), (0, 2), (1, 1), (0, 1))[n - 1]
            pass_on(1, k, r, away)
            pass_on(-1, k, 1 - r, away)

    near = 1 - 2 * zl
    blocks = [h, wrap(h - near, SIDE), wrap(h + near, SIDE), wrap(h + 2, SIDE)]
    early, late = tuple(blocks[:2]), tuple(blocks[2:])
    relay_acts("b", 2, 0)
    from_partner("early", 0)
    encode(0, early)
    relay_acts("a", 2, 1)
    decode(0, early)
    from_partner("late", 0)
    encode(0, late)
    decode(0, late)
    relay_acts("b", 1, 1)
    from_partner("early", 1)
    encode(1, early)
    decoded(0)
    steps(0, 1, 2)
    decode(1, early)
    relay_acts("b", 2, 1)
    norms = []
    for q in range(2):
        rows_q = wdec[2 * q : 2 * q + 2].reshape(LAT // 2, D).astype(F32)
        norms.append(jnp.sqrt(jnp.sum(rows_q * rows_q, axis=1, keepdims=True) + 1e-06))
    norms = jnp.concatenate(norms, axis=0)
    from_partner("late", 1)
    encode(1, late)
    decode(1, late)
    steps(0, 3, 4)
    decoded(1)
    for n, m in ((1, 5), (2, 6)):
        steps(1, n)
        steps(0, m)
    steps(0, 7)
    steps(1, 3, 4)

    own_rows = zl * PORTION + c * SUB

    def at_home(k):
        for r in range(2):
            at = k * CH + r * STRIP
            here = pl.ds(pl.multiple_of(own_rows + at, STRIP), STRIP)
            total = part_sum(k, z, r) + dbias[...]
            arrive(rsp.at[k, 0, strip(r)], sems("rp", k, r, 1))
            arrive(rsm.at[k, 0, strip(r)], sems("rm", k, r, 1))
            full = total + rsp[k, 0, strip(r)].astype(F32) + rsm[k, 0, strip(r)].astype(F32)
            rec[here] = full.astype(BF16)
            err[k, z, c, strip(r)] = (full - acts[here]).astype(BF16)
            mine = rows(err, z, k).at[strip(r)]
            send(mine, mine, sems("gp", 0, k, r), at_z(1), "err")
            send(mine, mine, sems("gm", 0, k, r), at_z(-1), "err")
            send(mine, mine, sems("errc", 0, 0), partner, "errc")

    at_home(0)
    steps(1, 5, 6, 7)

    def incoming(s, k, r, sign, core=None):
        return rows(err, wrap(z - sign * (s + 1), NZ), k, core).at[strip(r)]

    def relay_err(s, k):
        for r in range(2):
            for sign, name in ((1, "gp"), (-1, "gm")):
                if s == 3 and not farthest(sign, r):
                    continue
                part = incoming(s, k, r, sign)
                arrive(part, sems(name, s, k, r))
                if s < 2 or (s == 2 and farthest(sign, r)):
                    send(part, part, sems(name, s + 1, k, r), at_z(sign), "err")
                send(part, part, sems("errc", s, k if s == 3 else 0), partner, "errc")

    def err_from_partner(s, k=0):
        arrive(err.at[0, 0, 0] if s == 3 else err.at[0, pl.ds(0, (3, 2, 2)[s])], sems("errc", s, k))

    def backward(b, first, last, half=None):
        ks, n = (slice(None), ROWS) if half is None else (pl.ds(half, 1), PORTION)
        block = err[ks, pl.ds(2 * b, 2)].reshape(n, D)
        weights = wdec[...].reshape(LAT, D)
        back = lax.dot_general(weights, block, NT, preferred_element_type=F32)
        kept = jnp.concatenate([codes_t[0, b], codes_t[1, b]], axis=1) if half is None else codes_t[half, b]
        grad_pre = jnp.where(kept.astype(F32) > 0.0, back + SPARSITY * norms, 0.0)
        folded = grad_pre[:, :128] + grad_pre[:, 128:] if half is None else grad_pre
        gb[...] = folded if first else gb[...] + folded
        grad_bf = grad_pre.astype(BF16)
        if last:
            pay_e[:, :, :, :128] = gb[...].astype(BF16).reshape(SIDE, SIDE, OWN, 128)
            pay_e[:, :, :, 128:STATS] = cs[...].astype(BF16).reshape(SIDE, SIDE, OWN, 128)
        for left, data, acc, pay in ((grad_bf, cent, acc_e, pay_e), (kept, err, acc_d, pay_d)):
            for t in range(0, D, TILE):
                right = data[ks, pl.ds(2 * b, 2), :, :, t : t + TILE].reshape(n, TILE)
                total = jnp.dot(left, right, preferred_element_type=F32)
                if not first:
                    total = total + acc[:, t : t + TILE]
                if not last:
                    acc[:, t : t + TILE] = total
                    continue
                at = t + (STATS if pay is pay_e else 0)
                pay[:, :, :, at : at + TILE] = total.astype(BF16).reshape(SIDE, SIDE, OWN, TILE)
                if t % (D // 2) == D // 2 - TILE:
                    (start_e if pay is pay_e else start_d)(2 * t // D)

    low, high = pl.ds(0, 2), pl.ds(2, 2)

    def e_part(yy, half, cols):
        return pay_e.at[yy, half, :, cols]

    def d_part(xx, half, cols):
        return pay_d.at[half, xx, :, cols]

    E_COLS = [pl.ds(0, STATS + D // 2), pl.ds(STATS + D // 2, D // 2)]
    D_COLS = [pl.ds(0, D // 2), pl.ds(D // 2, D // 2)]

    def start(i, cols, part, v, far, close, name, at):
        for n, s, summed, plain in ((0, 1, low, high), (1, -1, high, low)):
            send(part(wrap(v + 2, SIDE), summed, cols), far.at[n, :, :, cols], sems(name, "far", s, i), at(s), (name, i))
        for n, s, summed, plain in ((0, 1, low, high), (1, -1, high, low)):
            send(part(wrap(v + s, SIDE), plain, cols), close.at[n, plain, :, cols], sems(name, "near", i), at(s), (name, i))

    def start_e(i):
        start(i, E_COLS[i], e_part, y, e_far, e_near, "e", at_y)

    def start_d(i):
        start(i, D_COLS[i], d_part, x, d_far, d_near, "d", at_x)

    def forward_sum(i, cols, part, v, far, close, name, at):
        for n, s, half in ((0, 1, low), (1, -1, high)):
            arrive(far.at[n, :, :, cols], sems(name, "far", s, i))
            block = part(wrap(v + s, SIDE), half, cols)
            block[...] = (block[...].astype(F32) + far[n, :, :, cols].astype(F32)).astype(BF16)
            send(block, close.at[n, half, :, cols], sems(name, "near", i), at(s), (name, i))

    def at_owner(i, cols, part, v, w, close, tot, last, name, at):
        arrive(close.at[:, :, :, cols], sems(name, "near", i))
        tot[:, :, cols] = (
            part(v, pl.ds(0, SIDE), cols)[...].astype(F32)
            + close[0, :, :, cols].astype(F32)
            + close[1, :, :, cols].astype(F32)
        ).astype(BF16)
        for d in (2, 1, 3):
            send(tot.at[wrap(w + d, SIDE), :, cols], last.at[d - 1, :, cols], sems(name, "last", i), at(d), (name, "last", i))

    def owned(i, cols, w, tot, last, name):
        total = tot[w, :, cols].astype(F32)
        arrive(last.at[:, :, cols], sems(name, "last", i))
        for d in (1, 2, 3):
            total = total + last[d - 1, :, cols].astype(F32)
        return total

    relay_err(0, 0)
    at_home(1)
    relay_err(1, 0)
    relay_err(0, 1)
    relay_err(2, 0)
    relay_err(1, 1)
    err_from_partner(0)
    backward(blocks[0], True, False)
    relay_err(3, 0)
    err_from_partner(1)
    backward(blocks[1], False, False)
    relay_err(2, 1)
    err_from_partner(2)
    backward(blocks[2], False, False)
    err_from_partner(3, 0)
    backward(blocks[3], False, False, 0)
    relay_err(3, 1)
    own_rec = rec.at[pl.ds(pl.multiple_of(own_rows, SUB), SUB)]
    send(own_rec, own_rec, sems("rc"), partner, "rec")
    send(own_rec, own_rec, sems("rz"), pair, "rec")
    err_from_partner(3, 1)
    backward(blocks[3], False, True, 1)

    for i in range(2):
        forward_sum(i, E_COLS[i], e_part, y, e_far, e_near, "e", at_y)
        forward_sum(i, D_COLS[i], d_part, x, d_far, d_near, "d", at_x)
    pair_rec = rec.at[pl.ds(pl.multiple_of((1 - zl) * PORTION + c * SUB, SUB), SUB)]
    arrive(pair_rec, sems("rz"))
    send(pair_rec, pair_rec, sems("rc"), partner, "rec")
    for i in range(2):
        at_owner(i, E_COLS[i], e_part, y, x, e_near, tot_e, e_last, "e", at_x)
        at_owner(i, D_COLS[i], d_part, x, y, d_near, tot_d, d_last, "d", at_y)
    arrive(rec.at[pl.ds(0, 2 * SUB)], sems("rc"))
    recon[...] = rec[...]

    scale = (ROWS * SIDE * SIDE * SIDE) ** -0.5
    mine = dec[...].astype(F32)
    own_norms = jnp.sqrt(jnp.sum(mine * mine, axis=1, keepdims=True) + 1e-06)
    sides = [pl.ds(0, D // 2), pl.ds(D // 2, D // 2)]
    for i in range(2):
        total = owned(i, E_COLS[i], x, tot_e, e_last, "e")
        genc[:, sides[i]] = scale * (total[:, STATS:] if i == 0 else total)
        if i == 0:
            bias_sums = scale * jnp.sum(total[:, :128], axis=1, keepdims=True)
            gbias[...] = jnp.sum(jnp.where(eye, bias_sums, 0.0), axis=0, keepdims=True)
            sparse = SPARSITY * jnp.sum(total[:, 128:STATS], axis=1, keepdims=True) * mine / own_norms
        total = owned(i, D_COLS[i], y, tot_d, d_last, "d")
        gdec[:, sides[i]] = scale * (total + sparse[:, i * (D // 2) : (i + 1) * (D // 2)])

    left(wenc.at[0, pl.ds(0, 3)], "we1")
    left(wdec.at[0, pl.ds(0, 3)], "wd1")
    left(wenc.at[pl.ds(0, 3)], "we2")
    left(wdec.at[pl.ds(0, 3)], "wd2")
    left(cent.at[:, pl.ds(0, 6)], "acts")
    left(cent.at[0], "px")
    left(cent.at[0, pl.ds(0, 7)], "sums")
    left(cent.at[0, pl.ds(0, 7)], "err")
    left(cent.at[0], "errc")
    left(rec.at[pl.ds(0, 3 * SUB)], "rec")
    for i in range(2):
        left(pay_e.at[pl.ds(0, 3), :, :, E_COLS[i]], ("e", i))
        left(pay_d.at[pl.ds(0, 3), :, :, D_COLS[i]], ("d", i))
        left(tot_e.at[pl.ds(0, 3), :, E_COLS[i]], ("e", "last", i))
        left(tot_d.at[pl.ds(0, 3), :, D_COLS[i]], ("d", "last", i))
    assert (len(sems.names), len(kinds.names)) == (N_ARRIVE, N_LEAVE)


def store(*refs):
    sources, results, sem = refs[:4], refs[4:8], refs[8]
    copies = [pltpu.make_async_copy(a, b, sem.at[i]) for i, (a, b) in enumerate(zip(sources, results))]
    for cp in copies:
        cp.start()
    for cp in copies:
        cp.wait()


def per_device(acts, dec_bias, enc_weight, enc_bias, dec_weight):
    vmem, anywhere = pl.BlockSpec(memory_space=pltpu.VMEM), pl.BlockSpec(memory_space=pl.ANY)
    results = (((ROWS, D), BF16), ((OWN, D), F32), ((OWN, D), F32), ((1, OWN), F32))
    in_vmem = pl.pallas_call(
        kernel,
        name="step",
        out_shape=tuple(pltpu.VMEM(*r) for r in results),
        in_specs=[anywhere] * 5,
        out_specs=(vmem,) * 4,
        scratch_shapes=[
            pltpu.VMEM((ROWS, D), F32),
            pltpu.VMEM((1, D), F32),
            pltpu.VMEM((1, OWN), BF16),
            pltpu.VMEM((OWN, D), BF16),
            pltpu.VMEM((2, NZ, 2, CH, D), BF16),
            pltpu.VMEM((SIDE, SIDE, OWN, WE), BF16),
            pltpu.VMEM((SIDE, SIDE, OWN, D), BF16),
            pltpu.VMEM((2, SIDE, 2, SUB, LAT), BF16),
            pltpu.VMEM((2, SIDE, LAT, PORTION), BF16),
            pltpu.VMEM((2, NZ, CH, D), F32),
            pltpu.VMEM((2, NZ, CH, D), BF16),
            pltpu.VMEM((2, NZ, CH, D), BF16),
            pltpu.VMEM((2, NZ, CH, D), BF16),
            pltpu.VMEM((2, 4, CH, D), BF16),
            pltpu.VMEM((2, 4, CH, D), BF16),
            pltpu.VMEM((2, NZ, 2, CH, D), BF16),
            pltpu.VMEM((LAT, D), F32),
            pltpu.VMEM((LAT, D), F32),
            pltpu.VMEM((LAT, 128), F32),
            pltpu.VMEM((LAT, 128), F32),
            pltpu.VMEM((SIDE, SIDE, OWN, GE), BF16),
            pltpu.VMEM((SIDE, SIDE, OWN, D), BF16),
            pltpu.VMEM((2, 2, OWN, GE), BF16),
            pltpu.VMEM((2, SIDE, OWN, GE), BF16),
            pltpu.VMEM((SIDE, OWN, GE), BF16),
            pltpu.VMEM((3, OWN, GE), BF16),
            pltpu.VMEM((2, 2, OWN, D), BF16),
            pltpu.VMEM((2, SIDE, OWN, D), BF16),
            pltpu.VMEM((SIDE, OWN, D), BF16),
            pltpu.VMEM((3, OWN, D), BF16),
            pltpu.VMEM((ROWS, D), BF16),
            pltpu.SemaphoreType.DMA((5,)),
            pltpu.SemaphoreType.DMA((N_LEAVE,)),
            pltpu.SemaphoreType.DMA((N_ARRIVE,)),
        ],
        compiler_params=pltpu.CompilerParams(collective_id=0, has_side_effects=True, vmem_limit_bytes=60 << 20),
    )(acts, dec_bias[None, :], enc_weight, enc_bias[None, :], dec_weight)
    recon, genc, gdec, gbias = pl.pallas_call(
        store,
        name="store",
        out_shape=tuple(jax.ShapeDtypeStruct(*r) for r in results),
        in_specs=[vmem] * 4,
        out_specs=(anywhere,) * 4,
        scratch_shapes=[pltpu.SemaphoreType.DMA((4,))],
    )(*[pltpu.with_memory_space_constraint(r, pltpu.VMEM) for r in in_vmem])
    return recon, genc, gdec, gbias[0]


def solution(mesh):
    torus = Mesh(mesh.devices.reshape(2, 2, SIDE, SIDE, SIDE), AXES)
    wide = P(("y", "x", "h"), None)
    return jax.shard_map(
        per_device,
        mesh=torus,
        in_specs=(wide, P(), P(AXES, None), P(AXES), P(AXES, None)),
        out_specs=(wide, P(AXES, None), P(AXES, None), P(AXES)),
        check_vma=False,
    )
```

```python
import jax
import jax.numpy as jnp
from jax import lax
from jax.experimental import pallas as pl
from jax.experimental.pallas import tpu as pltpu
from jax.sharding import Mesh
from jax.sharding import PartitionSpec as P


AXES = ("zl", "c", "y", "x", "h")
MESH = pl.DeviceIdType.MESH
F32, BF16 = jnp.float32, jnp.bfloat16
SPARSITY = 0.5
NZ, SIDE, ROWS, D, OWN, LAT = 8, 4, 256, 2048, 16, 256
PORTION = ROWS // 2
SUB = PORTION // 2
CH = SUB // 2
STRIP = CH // 2
WE = D + 128
STATS = 256
GE = STATS + D
TILE = 512


class Semaphores:
    def __init__(self):
        self.names = {}

    def __call__(self, *name):
        return self.names.setdefault(name, len(self.names))


N_ARRIVE, N_LEAVE = 105, 18
NT = (((1,), (1,)), ((), ()))


def kernel(
    acts_hbm, dbias_hbm, enc_hbm, bias_hbm, dec_hbm, recon, genc, gdec, gbias, acts, dbias, bias, dec,
    cent, wenc, wdec, codes, codes_t, pown, psend, precv, psum, rsp, rsm, err, acc_e, acc_d, gb, cs,
    pay_e, pay_d, e_far, e_near, tot_e, e_last, d_far, d_near, tot_d, d_last, rec, lsem, ssem, rsem,
):
    zl, c, y, x, h = [lax.axis_index(a) for a in AXES]
    z = 2 * h + zl
    sems, kinds = Semaphores(), Semaphores()

    def wrap(v, n):
        return lax.rem(v + 2 * n, n)

    def at_z(dz):
        q = wrap(z + dz, NZ)
        return (lax.rem(q, 2), c, y, x, lax.div(q, 2))

    def at_y(dy):
        return (zl, c, wrap(y + dy, SIDE), x, h)

    def at_x(dx):
        return (zl, c, y, wrap(x + dx, SIDE), h)

    partner = (zl, 1 - c, y, x, h)
    pair = (1 - zl, c, y, x, h)

    def copy(src, dst, dev, leaves, arrives):
        return pltpu.make_async_remote_copy(
            src_ref=src, dst_ref=dst, send_sem=ssem.at[leaves], recv_sem=rsem.at[arrives], device_id=dev, device_id_type=MESH
        )

    def send(src, dst, arrives, dev, kind):
        copy(src, dst, dev, kinds(kind), arrives).start()

    def arrive(dst, sem):
        copy(dst, dst, partner, 0, sem).wait_recv()

    def left(src, kind):
        copy(src, src, partner, kinds(kind), 0).wait_send()

    def rows(ref, p, k, core=None):
        return ref.at[k, p, c if core is None else core]

    loads = [
        pltpu.make_async_copy(src, dst, lsem.at[i])
        for i, (src, dst) in enumerate(
            (
                (bias_hbm, bias),
                (enc_hbm, wenc.at[y, x, :, pl.ds(0, D)]),
                (dec_hbm, dec),
                (dbias_hbm, dbias),
                (acts_hbm, acts),
            )
        )
    ]
    for load in loads:
        load.start()
    barrier = pltpu.get_barrier_semaphore()
    friends = [partner, at_z(1), at_z(-1)] + [at_y(d) for d in (1, 2, 3)] + [at_x(d) for d in (1, 2, 3)]
    for f in friends:
        pl.semaphore_signal(barrier, inc=1, device_id=f, device_id_type=MESH)
    for load in loads:
        load.wait()
    for q in range(2):
        for who in range(2):
            for k in range(2):
                at = q * PORTION + who * SUB + k * CH
                cent[k, 2 * h + q, who] = (acts[at : at + CH] - dbias[...]).astype(BF16)
    eye = lax.broadcasted_iota(jnp.int32, (OWN, OWN), 0) == lax.broadcasted_iota(jnp.int32, (OWN, OWN), 1)
    column = jnp.sum(jnp.where(eye, bias[...].astype(F32), 0.0), axis=1, keepdims=True)
    wenc[y, x, :, D:] = jnp.broadcast_to(column, (OWN, 128)).astype(BF16)
    wdec[y, x] = dec[...]
    pl.semaphore_wait(barrier, len(friends))

    for d in (1, 2, 3):
        send(wenc.at[y, x], wenc.at[y, x], sems("we1"), at_x(d), "we1")
        send(dec, wdec.at[y, x], sems("wd1"), at_y(d), "wd1")

    def mirrored(even, odd):
        return wrap(2 * h + even + zl * (odd - even), NZ)

    coming = {
        "a": [mirrored(-2, 3), mirrored(-1, 2), mirrored(-4, 5)],
        "b": [mirrored(3, -2), mirrored(2, -1), mirrored(5, -4)],
    }
    outer = at_z(2 * zl - 1)

    def piece(p, k):
        return rows(cent, p, k)

    def send_own(j, k):
        part = piece(mirrored(1 - j, j), k)
        send(part, part, sems("a", j, k), outer, "acts")

    send_own(0, 0)
    send_own(1, 0)
    send_own(0, 1)

    def relay_acts(name, j, k):
        part = piece(coming[name][j], k)
        arrive(part, sems(name, j, k))
        if name == "a":
            send(part, part, sems("b", j, k), pair, "acts")
        elif j == 0:
            send(part, part, sems("a", 2, k), outer, "acts")
        send(part, part, sems("early" if name == "a" and j < 2 else "late", k), partner, "acts")

    def from_partner(which, k):
        arrive(cent.at[0, pl.ds(0, 1 if which == "early" else 2)], sems(which, k))

    relay_acts("a", 0, 0)
    arrive(wenc.at[0, pl.ds(0, 3)], sems("we1"))
    arrive(wdec.at[0, pl.ds(0, 3)], sems("wd1"))
    for i in range(2):
        for s in (1, -1):
            half = pl.ds(0 if (s == 1) == (i == 0) else 2, 2)
            order = s if i == 0 else 0
            send(wenc.at[y, half], wenc.at[y, half], sems("we2", order), at_y(s), "we2")
            send(wdec.at[half, x], wdec.at[half, x], sems("wd2", order), at_x(s), "wd2")
    relay_acts("a", 1, 0)
    relay_acts("b", 0, 0)
    send_own(1, 1)
    relay_acts("a", 0, 1)
    relay_acts("b", 1, 0)
    for s in (1, -1):
        half = pl.ds(0 if s == 1 else 2, 2)
        yn, xn = wrap(y - s, SIDE), wrap(x - s, SIDE)
        arrive(wenc.at[yn, half], sems("we2", s))
        send(wenc.at[yn, half], wenc.at[yn, half], sems("we2", 0), at_y(s), "we2")
        arrive(wdec.at[half, xn], sems("wd2", s))
        send(wdec.at[half, xn], wdec.at[half, xn], sems("wd2", 0), at_x(s), "wd2")
    relay_acts("a", 2, 0)
    relay_acts("b", 0, 1)
    relay_acts("a", 1, 1)
    arrive(wenc.at[pl.ds(0, 2)], sems("we2", 0))
    arrive(wdec.at[pl.ds(0, 2)], sems("wd2", 0))

    def encode(k, pair_of):
        block = jnp.concatenate([cent[k, pl.ds(2 * b, 2)].reshape(PORTION, D) for b in pair_of], axis=0)
        weights = wenc[:, :, :, :D].reshape(LAT, D)
        shift = wenc[:, :, :, D:].reshape(LAT, 128).astype(F32)
        pre = lax.dot_general(weights, block, NT, preferred_element_type=F32)
        value = jnp.maximum(pre + jnp.concatenate([shift, shift], axis=1), 0.0)
        turned = value.T.astype(BF16)
        for i, b in enumerate(pair_of):
            for q in range(2):
                for who in range(2):
                    at = i * PORTION + q * SUB + who * CH
                    codes[k, b, who, q * CH : (q + 1) * CH] = turned[at : at + CH]
            codes_t[k, b] = value[:, i * PORTION : (i + 1) * PORTION].astype(BF16)
        folded = value[:, :128] + value[:, 128:]
        cs[...] = folded if k == 0 and pair_of is early else cs[...] + folded

    def decode(k, pair_of):
        left = [jnp.concatenate([codes[k, b, who] for b in pair_of], axis=0) for who in (1 - c, c)]
        for t in range(0, D, TILE):
            right = wdec[:, :, :, t : t + TILE].reshape(LAT, TILE)
            other = jnp.dot(left[0], right, preferred_element_type=F32).astype(BF16)
            mine = jnp.dot(left[1], right, preferred_element_type=F32)
            for i, b in enumerate(pair_of):
                for q in range(2):
                    r = slice((2 * i + q) * CH, (2 * i + q + 1) * CH)
                    psend[k, 2 * b + q, :, t : t + TILE] = other[r]
                    pown[k, 2 * b + q, :, t : t + TILE] = mine[r]
        for i, b in enumerate(pair_of):
            for q in range(2):
                part = precv.at[k, 2 * b + q]
                send(psend.at[k, 2 * b + q], part, sems("px", k), partner, "px")

    def decoded(k):
        arrive(precv.at[k], sems("px", k))

    def strip(r):
        return pl.ds(r * STRIP, STRIP)

    def farthest(sign, r):
        return (sign == 1) == (r == 0)

    def part_sum(k, p, r):
        return pown[k, p, strip(r)] + precv[k, p, strip(r)].astype(F32)

    def pass_on(sign, k, r, away):
        buf, name = (rsp, "rp") if sign == 1 else (rsm, "rm")
        p = wrap(z + sign * away, NZ)
        part = psum.at[k, p, strip(r)]
        total = part_sum(k, p, r)
        if away < (4 if farthest(sign, r) else 3):
            arrive(buf.at[k, away, strip(r)], sems(name, k, r, away + 1))
            total = total + buf[k, away, strip(r)].astype(F32)
        part[...] = total.astype(BF16)
        send(part, buf.at[k, away - 1, strip(r)], sems(name, k, r, away), at_z(sign), "sums")

    def steps(k, *which):
        for n in which:
            r, away = ((0, 4), (1, 3), (0, 3), (1, 2), (0, 2), (1, 1), (0, 1))[n - 1]
            pass_on(1, k, r, away)
            pass_on(-1, k, 1 - r, away)

    near = 1 - 2 * zl
    blocks = [h, wrap(h - near, SIDE), wrap(h + near, SIDE), wrap(h + 2, SIDE)]
    early, late = tuple(blocks[:2]), tuple(blocks[2:])
    relay_acts("b", 2, 0)
    from_partner("early", 0)
    encode(0, early)
    relay_acts("a", 2, 1)
    decode(0, early)
    from_partner("late", 0)
    encode(0, late)
    decode(0, late)
    relay_acts("b", 1, 1)
    from_partner("early", 1)
    encode(1, early)
    decoded(0)
    steps(0, 1, 2)
    decode(1, early)
    relay_acts("b", 2, 1)
    norms = []
    for q in range(2):
        rows_q = wdec[2 * q : 2 * q + 2].reshape(LAT // 2, D).astype(F32)
        norms.append(jnp.sqrt(jnp.sum(rows_q * rows_q, axis=1, keepdims=True) + 1e-06))
    norms = jnp.concatenate(norms, axis=0)
    from_partner("late", 1)
    encode(1, late)
    decode(1, late)
    steps(0, 3, 4)
    decoded(1)
    for n, m in ((1, 5), (2, 6)):
        steps(1, n)
        steps(0, m)
    steps(0, 7)
    steps(1, 3, 4)

    own_rows = zl * PORTION + c * SUB

    def at_home(k):
        for r in range(2):
            at = k * CH + r * STRIP
            here = pl.ds(pl.multiple_of(own_rows + at, STRIP), STRIP)
            total = part_sum(k, z, r) + dbias[...]
            arrive(rsp.at[k, 0, strip(r)], sems("rp", k, r, 1))
            arrive(rsm.at[k, 0, strip(r)], sems("rm", k, r, 1))
            full = total + rsp[k, 0, strip(r)].astype(F32) + rsm[k, 0, strip(r)].astype(F32)
            rec[here] = full.astype(BF16)
            err[k, z, c, strip(r)] = (full - acts[here]).astype(BF16)
            mine = rows(err, z, k).at[strip(r)]
            send(mine, mine, sems("gp", 0, k, r), at_z(1), "err")
            send(mine, mine, sems("gm", 0, k, r), at_z(-1), "err")
            send(mine, mine, sems("errc", 0, 0), partner, "errc")

    at_home(0)
    steps(1, 5, 6, 7)

    def incoming(s, k, r, sign, core=None):
        return rows(err, wrap(z - sign * (s + 1), NZ), k, core).at[strip(r)]

    def relay_err(s, k):
        for r in range(2):
            for sign, name in ((1, "gp"), (-1, "gm")):
                if s == 3 and not farthest(sign, r):
                    continue
                part = incoming(s, k, r, sign)
                arrive(part, sems(name, s, k, r))
                if s < 2 or (s == 2 and farthest(sign, r)):
                    send(part, part, sems(name, s + 1, k, r), at_z(sign), "err")
                send(part, part, sems("errc", s, k if s == 3 else 0), partner, "errc")

    def err_from_partner(s, k=0):
        arrive(err.at[0, 0, 0] if s == 3 else err.at[0, pl.ds(0, (3, 2, 2)[s])], sems("errc", s, k))

    def backward(b, first, last, half=None):
        ks, n = (slice(None), ROWS) if half is None else (pl.ds(half, 1), PORTION)
        block = err[ks, pl.ds(2 * b, 2)].reshape(n, D)
        weights = wdec[...].reshape(LAT, D)
        back = lax.dot_general(weights, block, NT, preferred_element_type=F32)
        kept = jnp.concatenate([codes_t[0, b], codes_t[1, b]], axis=1) if half is None else codes_t[half, b]
        grad_pre = jnp.where(kept.astype(F32) > 0.0, back + SPARSITY * norms, 0.0)
        folded = grad_pre[:, :128] + grad_pre[:, 128:] if half is None else grad_pre
        gb[...] = folded if first else gb[...] + folded
        grad_bf = grad_pre.astype(BF16)
        if last:
            pay_e[:, :, :, :128] = gb[...].astype(BF16).reshape(SIDE, SIDE, OWN, 128)
            pay_e[:, :, :, 128:STATS] = cs[...].astype(BF16).reshape(SIDE, SIDE, OWN, 128)
        for left, data, acc, pay in ((grad_bf, cent, acc_e, pay_e), (kept, err, acc_d, pay_d)):
            for t in range(0, D, TILE):
                right = data[ks, pl.ds(2 * b, 2), :, :, t : t + TILE].reshape(n, TILE)
                total = jnp.dot(left, right, preferred_element_type=F32)
                if not first:
                    total = total + acc[:, t : t + TILE]
                if not last:
                    acc[:, t : t + TILE] = total
                    continue
                at = t + (STATS if pay is pay_e else 0)
                pay[:, :, :, at : at + TILE] = total.astype(BF16).reshape(SIDE, SIDE, OWN, TILE)
                if t % (D // 2) == D // 2 - TILE:
                    (start_e if pay is pay_e else start_d)(2 * t // D)

    low, high = pl.ds(0, 2), pl.ds(2, 2)

    def e_part(yy, half, cols):
        return pay_e.at[yy, half, :, cols]

    def d_part(xx, half, cols):
        return pay_d.at[half, xx, :, cols]

    E_COLS = [pl.ds(0, STATS + D // 2), pl.ds(STATS + D // 2, D // 2)]
    D_COLS = [pl.ds(0, D // 2), pl.ds(D // 2, D // 2)]

    def start(i, cols, part, v, far, close, name, at):
        for n, s, summed, plain in ((0, 1, low, high), (1, -1, high, low)):
            send(part(wrap(v + 2, SIDE), summed, cols), far.at[n, :, :, cols], sems(name, "far", s, i), at(s), (name, i))
        for n, s, summed, plain in ((0, 1, low, high), (1, -1, high, low)):
            send(part(wrap(v + s, SIDE), plain, cols), close.at[n, plain, :, cols], sems(name, "near", i), at(s), (name, i))

    def start_e(i):
        start(i, E_COLS[i], e_part, y, e_far, e_near, "e", at_y)

    def start_d(i):
        start(i, D_COLS[i], d_part, x, d_far, d_near, "d", at_x)

    def forward_sum(i, cols, part, v, far, close, name, at):
        for n, s, half in ((0, 1, low), (1, -1, high)):
            arrive(far.at[n, :, :, cols], sems(name, "far", s, i))
            block = part(wrap(v + s, SIDE), half, cols)
            block[...] = (block[...].astype(F32) + far[n, :, :, cols].astype(F32)).astype(BF16)
            send(block, close.at[n, half, :, cols], sems(name, "near", i), at(s), (name, i))

    def at_owner(i, cols, part, v, w, close, tot, last, name, at):
        arrive(close.at[:, :, :, cols], sems(name, "near", i))
        tot[:, :, cols] = (
            part(v, pl.ds(0, SIDE), cols)[...].astype(F32)
            + close[0, :, :, cols].astype(F32)
            + close[1, :, :, cols].astype(F32)
        ).astype(BF16)
        for d in (2, 1, 3):
            send(tot.at[wrap(w + d, SIDE), :, cols], last.at[d - 1, :, cols], sems(name, "last", i), at(d), (name, "last", i))

    def owned(i, cols, w, tot, last, name):
        total = tot[w, :, cols].astype(F32)
        arrive(last.at[:, :, cols], sems(name, "last", i))
        for d in (1, 2, 3):
            total = total + last[d - 1, :, cols].astype(F32)
        return total

    relay_err(0, 0)
    at_home(1)
    relay_err(1, 0)
    relay_err(0, 1)
    relay_err(2, 0)
    relay_err(1, 1)
    err_from_partner(0)
    backward(blocks[0], True, False)
    relay_err(2, 1)
    relay_err(3, 0)
    err_from_partner(1)
    backward(blocks[1], False, False)
    err_from_partner(2)
    backward(blocks[2], False, False)
    err_from_partner(3, 0)
    backward(blocks[3], False, False, 0)
    relay_err(3, 1)
    own_rec = rec.at[pl.ds(pl.multiple_of(own_rows, SUB), SUB)]
    send(own_rec, own_rec, sems("rc"), partner, "rec")
    send(own_rec, own_rec, sems("rz"), pair, "rec")
    err_from_partner(3, 1)
    backward(blocks[3], False, True, 1)

    for i in range(2):
        forward_sum(i, E_COLS[i], e_part, y, e_far, e_near, "e", at_y)
        forward_sum(i, D_COLS[i], d_part, x, d_far, d_near, "d", at_x)
    pair_rec = rec.at[pl.ds(pl.multiple_of((1 - zl) * PORTION + c * SUB, SUB), SUB)]
    arrive(pair_rec, sems("rz"))
    send(pair_rec, pair_rec, sems("rc"), partner, "rec")
    for i in range(2):
        at_owner(i, E_COLS[i], e_part, y, x, e_near, tot_e, e_last, "e", at_x)
        at_owner(i, D_COLS[i], d_part, x, y, d_near, tot_d, d_last, "d", at_y)
    arrive(rec.at[pl.ds(0, 2 * SUB)], sems("rc"))
    recon[...] = rec[...]

    scale = (ROWS * SIDE * SIDE * SIDE) ** -0.5
    mine = dec[...].astype(F32)
    own_norms = jnp.sqrt(jnp.sum(mine * mine, axis=1, keepdims=True) + 1e-06)
    sides = [pl.ds(0, D // 2), pl.ds(D // 2, D // 2)]
    for i in range(2):
        total = owned(i, E_COLS[i], x, tot_e, e_last, "e")
        genc[:, sides[i]] = scale * (total[:, STATS:] if i == 0 else total)
        if i == 0:
            bias_sums = scale * jnp.sum(total[:, :128], axis=1, keepdims=True)
            gbias[...] = jnp.sum(jnp.where(eye, bias_sums, 0.0), axis=0, keepdims=True)
            sparse = SPARSITY * jnp.sum(total[:, 128:STATS], axis=1, keepdims=True) * mine / own_norms
        total = owned(i, D_COLS[i], y, tot_d, d_last, "d")
        gdec[:, sides[i]] = scale * (total + sparse[:, i * (D // 2) : (i + 1) * (D // 2)])

    left(wenc.at[0, pl.ds(0, 3)], "we1")
    left(wdec.at[0, pl.ds(0, 3)], "wd1")
    left(wenc.at[pl.ds(0, 3)], "we2")
    left(wdec.at[pl.ds(0, 3)], "wd2")
    left(cent.at[:, pl.ds(0, 6)], "acts")
    left(cent.at[0], "px")
    left(cent.at[0, pl.ds(0, 7)], "sums")
    left(cent.at[0, pl.ds(0, 7)], "err")
    left(cent.at[0], "errc")
    left(rec.at[pl.ds(0, 3 * SUB)], "rec")
    for i in range(2):
        left(pay_e.at[pl.ds(0, 3), :, :, E_COLS[i]], ("e", i))
        left(pay_d.at[pl.ds(0, 3), :, :, D_COLS[i]], ("d", i))
        left(tot_e.at[pl.ds(0, 3), :, E_COLS[i]], ("e", "last", i))
        left(tot_d.at[pl.ds(0, 3), :, D_COLS[i]], ("d", "last", i))
    assert (len(sems.names), len(kinds.names)) == (N_ARRIVE, N_LEAVE)


def store(*refs):
    sources, results, sem = refs[:4], refs[4:8], refs[8]
    copies = [pltpu.make_async_copy(a, b, sem.at[i]) for i, (a, b) in enumerate(zip(sources, results))]
    for cp in copies:
        cp.start()
    for cp in copies:
        cp.wait()


def per_device(acts, dec_bias, enc_weight, enc_bias, dec_weight):
    vmem, anywhere = pl.BlockSpec(memory_space=pltpu.VMEM), pl.BlockSpec(memory_space=pl.ANY)
    results = (((ROWS, D), BF16), ((OWN, D), F32), ((OWN, D), F32), ((1, OWN), F32))
    in_vmem = pl.pallas_call(
        kernel,
        name="step",
        out_shape=tuple(pltpu.VMEM(*r) for r in results),
        in_specs=[anywhere] * 5,
        out_specs=(vmem,) * 4,
        scratch_shapes=[
            pltpu.VMEM((ROWS, D), F32),
            pltpu.VMEM((1, D), F32),
            pltpu.VMEM((1, OWN), BF16),
            pltpu.VMEM((OWN, D), BF16),
            pltpu.VMEM((2, NZ, 2, CH, D), BF16),
            pltpu.VMEM((SIDE, SIDE, OWN, WE), BF16),
            pltpu.VMEM((SIDE, SIDE, OWN, D), BF16),
            pltpu.VMEM((2, SIDE, 2, SUB, LAT), BF16),
            pltpu.VMEM((2, SIDE, LAT, PORTION), BF16),
            pltpu.VMEM((2, NZ, CH, D), F32),
            pltpu.VMEM((2, NZ, CH, D), BF16),
            pltpu.VMEM((2, NZ, CH, D), BF16),
            pltpu.VMEM((2, NZ, CH, D), BF16),
            pltpu.VMEM((2, 4, CH, D), BF16),
            pltpu.VMEM((2, 4, CH, D), BF16),
            pltpu.VMEM((2, NZ, 2, CH, D), BF16),
            pltpu.VMEM((LAT, D), F32),
            pltpu.VMEM((LAT, D), F32),
            pltpu.VMEM((LAT, 128), F32),
            pltpu.VMEM((LAT, 128), F32),
            pltpu.VMEM((SIDE, SIDE, OWN, GE), BF16),
            pltpu.VMEM((SIDE, SIDE, OWN, D), BF16),
            pltpu.VMEM((2, 2, OWN, GE), BF16),
            pltpu.VMEM((2, SIDE, OWN, GE), BF16),
            pltpu.VMEM((SIDE, OWN, GE), BF16),
            pltpu.VMEM((3, OWN, GE), BF16),
            pltpu.VMEM((2, 2, OWN, D), BF16),
            pltpu.VMEM((2, SIDE, OWN, D), BF16),
            pltpu.VMEM((SIDE, OWN, D), BF16),
            pltpu.VMEM((3, OWN, D), BF16),
            pltpu.VMEM((ROWS, D), BF16),
            pltpu.SemaphoreType.DMA((5,)),
            pltpu.SemaphoreType.DMA((N_LEAVE,)),
            pltpu.SemaphoreType.DMA((N_ARRIVE,)),
        ],
        compiler_params=pltpu.CompilerParams(collective_id=0, has_side_effects=True, vmem_limit_bytes=60 << 20),
    )(acts, dec_bias[None, :], enc_weight, enc_bias[None, :], dec_weight)
    recon, genc, gdec, gbias = pl.pallas_call(
        store,
        name="store",
        out_shape=tuple(jax.ShapeDtypeStruct(*r) for r in results),
        in_specs=[vmem] * 4,
        out_specs=(anywhere,) * 4,
        scratch_shapes=[pltpu.SemaphoreType.DMA((4,))],
    )(*[pltpu.with_memory_space_constraint(r, pltpu.VMEM) for r in in_vmem])
    return recon, genc, gdec, gbias[0]


def solution(mesh):
    torus = Mesh(mesh.devices.reshape(2, 2, SIDE, SIDE, SIDE), AXES)
    wide = P(("y", "x", "h"), None)
    return jax.shard_map(
        per_device,
        mesh=torus,
        in_specs=(wide, P(), P(AXES, None), P(AXES), P(AXES, None)),
        out_specs=(wide, P(AXES, None), P(AXES, None), P(AXES)),
        check_vma=False,
    )
```
